32 devices in a mesh: rep: 1, ep: 32 (over z, y, x, core), hid: 1.
Axes of the slice: x: 2, y: 2, z: 4, core: 2. Of those that a mesh axis runs over, the one named last changes fastest.
Arguments:
- tokens: bfloat16 [4096, 2048], P(('rep', 'ep')), may hold values from -6 to 6
- cotangent: bfloat16 [4096, 2048], P(('rep', 'ep')), may hold values from -2 to 2
- routing: float32 [4096, 8], P(('rep', 'ep')), may hold values from 0.05 to 0.5
- expert_ids: int32 [4096, 8], P(('rep', 'ep')), may hold values from 0 to 63, all different within a row; in each aligned block of 128 rows (0 to 127, 128 to 255, ...) at most 20 rows name the same one
- gate_weight: bfloat16 [64, 2048, 768], P('ep', None, 'hid'), may hold values from -0.125 to 0.125
- up_weight: bfloat16 [64, 2048, 768], P('ep', None, 'hid'), may hold values from -0.125 to 0.125
- down_weight: bfloat16 [64, 768, 2048], P('ep', 'hid'), may hold values from -0.21875 to 0.21875
Outputs:
- input_grad: float32 [4096, 2048], P(('rep', 'ep'), 'hid')
- gate_grad: float32 [4096, 8], P(('rep', 'ep'))
The draws below stay inside these ranges and needn't reach their ends.
Inputs may be any that keep to these rules, and one draw needn't show every extreme that they name: `expert_ids`: among the 128 tokens of one index of ep (aligned blocks of rows), no expert is picked more than 20 times, a bound that some block reaches; the 8 picks of a token are different experts.
All inputs are finite; a program needn't handle non-finite values.
Results may differ from the reference program's by a relative error of at most 0.0029.
Values may be sent and summed in bfloat16 or wider, within the bound.
A program may use at most 128 MiB of HBM per device.

```python
import math
import jax
import jax.numpy as jnp
import numpy as np
from jax import lax

D = 2048
FF = 768
TOP = 8
TOK_DEV = 128
EXPERTS = 64
TOKENS = 4096
CAP = 20
N_EP = 32


def levels(rng, shape, split, smallest, high):
    factor_of, own = 1.0, jax.random.fold_in(rng, 6)
    for position, parts in split:
        heights = jnp.exp(jax.random.uniform(jax.random.fold_in(own, position), (parts,), jnp.float32, smallest / len(split), high / len(split)))
        factor_of = factor_of * jnp.repeat(heights, shape[position] // parts).reshape([-1 if axis == position else 1 for axis in range(len(shape))])
    return factor_of


def deal_out(own_key, own, number, rows, count, top, bound, skew):
    ranking = jax.random.permutation(own_key, count)
    crowded, common = load_shares(count, rows * top, bound, skew, True), load_shares(count, rows * top, bound, skew, False)
    places = jnp.arange(count)

    def named(sizes, offset_by):
        used = int((sizes > 0).sum())
        fixed = max(1, used // 4)
        moved = fixed + (places - fixed + offset_by * (used - fixed)) % max(1, count - fixed)
        return jnp.zeros((count,), jnp.int32).at[ranking[jnp.where(places < fixed, places, moved)]].set(jnp.asarray(sizes, jnp.int32))

    sizes = jnp.where(number % 4 == 0, named(crowded, number // 4), named(common, number - number // 4 - 1))
    mixed = jax.random.permutation(jax.random.fold_in(own, 3), count)
    source_of, receiver = mixed[0:count // 2 * 2:2], mixed[1:count // 2 * 2:2]
    slack = jnp.minimum(sizes[source_of] - 1, bound - sizes[receiver]) // 2
    slack = jnp.where((source_of == ranking[0]) | (receiver == ranking[0]) | (sizes[receiver] == 0), 0, jnp.maximum(slack, 0))
    moved = jax.random.randint(jax.random.fold_in(own, 4), (count // 2,), 0, 1 << 20) % (slack + 1)
    sizes = sizes.at[source_of].add(-moved).at[receiver].add(moved)
    items = jnp.searchsorted(jnp.cumsum(sizes), jnp.arange(rows * top), side="right").astype(jnp.int32)
    table = items.reshape(top, rows).T
    table = table[jax.random.permutation(jax.random.fold_in(own, 1), rows)]
    offset_by = jax.random.randint(jax.random.fold_in(own, 2), (rows, 1), 0, top)
    return jnp.take_along_axis(table, (jnp.arange(top)[None, :] + offset_by) % top, axis=1)


def load_shares(number_of, total, most, lean, full):
    weights = [(1 << 20) // math.isqrt(rank ** lean) + 1 for rank in range(1, number_of + 1)]
    largest = most if full else min(most, max(-(-total // number_of), total * weights[0] // sum(weights)))
    least = 1 if total - largest >= number_of - 1 else 0
    holding, spare = [largest] + [least] * (number_of - 1), total - largest - least * (number_of - 1)
    while spare > 0:
        candidates = [i for i in range(1, number_of) if holding[i] < largest] or [i for i in range(1, number_of) if holding[i] < most]
        whole, left = sum([weights[i] for i in candidates]), spare
        for i in candidates:
            more = min(most - holding[i], max(1, left * weights[i] // whole), spare)
            holding[i] = holding[i] + more
            spare = spare - more
    return np.array(holding)


def bell_draw(rng, dims, deviation, bound, pieces=(), kind=jnp.bfloat16):
    gain = levels(rng, dims, pieces, -0.22, 0.18) if pieces else 1.0
    entries = jax.random.normal(rng, dims, jnp.float32) * deviation * gain
    return jnp.minimum(jnp.maximum(entries, -bound), bound).astype(kind)


def setup_inputs(seed: int = 0, part: int = 0) -> dict:
    arg_keys = jax.random.split(jax.random.key(seed), 8)
    own_keys = jax.random.split(jax.random.fold_in(arg_keys[7], part), 8)
    tokens = bell_draw(own_keys[0], (TOKENS, D), 1.0, 6.0, ((0, 32),))
    cotangent = bell_draw(own_keys[1], (TOKENS, D), 0.3, 2.0, ((0, 32),))
    routing = jnp.clip(jnp.exp(math.log(0.5) - 2.3025851 * jax.random.uniform(own_keys[2], (TOKENS, TOP), jnp.float32) ** levels(own_keys[2], (TOKENS, TOP), ((0, 32),), -0.2, 0.2)), 0.05, 0.5)
    expert_ids_keys = jax.random.split(jax.random.fold_in(own_keys[3], 1), TOKENS // TOK_DEV)
    expert_ids_turns = jax.random.permutation(jax.random.fold_in(own_keys[3], 3), TOKENS // TOK_DEV)
    expert_ids = jax.vmap(lambda own, number: deal_out(jax.random.fold_in(own_keys[3], 2), own, number, TOK_DEV, EXPERTS, TOP, CAP, 1))(expert_ids_keys, expert_ids_turns).reshape((TOKENS, TOP))
    gate_weight = bell_draw(arg_keys[4], (EXPERTS, D, FF), D ** -0.5, 0.125, ((0, 32),))
    up_weight = bell_draw(arg_keys[5], (EXPERTS, D, FF), D ** -0.5, 0.125, ((0, 32),))
    down_weight = bell_draw(arg_keys[6], (EXPERTS, FF, D), FF ** -0.5, 0.21875, ((0, 32),))
    return dict(tokens=tokens, cotangent=cotangent, routing=routing, expert_ids=expert_ids, gate_weight=gate_weight, up_weight=up_weight, down_weight=down_weight)


def slot_rank(flat, experts):
    onehot = (flat[:, None] == jnp.arange(experts, dtype=jnp.int32)[None, :]).astype(jnp.int32)
    before = jnp.cumsum(onehot, axis=0) - onehot
    return jnp.sum(before * onehot, axis=1).astype(jnp.int32)


def reference(tokens, cotangent, routing, expert_ids, gate_weight, up_weight, down_weight):
    picks = TOK_DEV * TOP
    rows_expert = N_EP * CAP
    id_blocks = expert_ids.reshape(N_EP, picks).astype(jnp.int32)
    ranks = jax.vmap(lambda flat: slot_rank(flat, EXPERTS))(id_blocks)
    source = jnp.arange(N_EP, dtype=jnp.int32)[:, None]
    slots = (id_blocks * rows_expert + source * CAP + ranks).reshape(-1).astype(jnp.int32)
    pick_index = jnp.arange(TOKENS * TOP, dtype=jnp.int32)
    token_index = (pick_index // TOP).astype(jnp.int32)
    slot_token = jnp.full((EXPERTS * rows_expert,), TOKENS, jnp.int32).at[slots].set(token_index)
    slot_pick = jnp.full((EXPERTS * rows_expert,), TOKENS * TOP, jnp.int32).at[slots].set(pick_index)
    padding = jnp.zeros((1, D), tokens.dtype)
    token_rows = jnp.concatenate([tokens, padding], 0)[slot_token].reshape(EXPERTS, rows_expert, D)
    cotan_rows = jnp.concatenate([cotangent, padding], 0)[slot_token].reshape(EXPERTS, rows_expert, D)
    weight_flat = jnp.concatenate([routing.reshape(-1), jnp.zeros((1,), jnp.float32)], 0)
    slot_weight = weight_flat[slot_pick].reshape(EXPERTS, rows_expert)
    slot_token = slot_token.reshape(EXPERTS, rows_expert)
    slot_pick = slot_pick.reshape(EXPERTS, rows_expert)

    def expert_step(carry, items):
        grad_sum, gate_sum = carry
        inputs, grads_in, w_gate, up_proj, w_down, target, pick_slot, weight = items
        gate_pre = jnp.dot(inputs, w_gate, preferred_element_type=jnp.float32)
        up_pre = jnp.dot(inputs, up_proj, preferred_element_type=jnp.float32)
        upward = jnp.dot(grads_in, w_down.T, preferred_element_type=jnp.float32)
        sigma = jax.nn.sigmoid(gate_pre)
        silu_val = gate_pre * sigma
        hidden = silu_val * up_pre
        pick_gate = jnp.sum(hidden * upward, axis=1)
        gate_delta = (upward * up_pre * sigma * (1.0 + gate_pre * (1.0 - sigma))).astype(jnp.bfloat16)
        up_delta = (upward * silu_val).astype(jnp.bfloat16)
        pick_grad = jnp.dot(gate_delta, w_gate.T, preferred_element_type=jnp.float32)
        pick_grad = pick_grad + jnp.dot(up_delta, up_proj.T, preferred_element_type=jnp.float32)
        grad_sum = grad_sum.at[target].add(weight[:, None] * pick_grad, mode="drop")
        gate_sum = gate_sum.at[pick_slot].add(pick_gate, mode="drop")
        return (grad_sum, gate_sum), None

    start = (jnp.zeros((TOKENS, D), jnp.float32), jnp.zeros((TOKENS * TOP,), jnp.float32))
    (grad_sum, gate_sum), _ = lax.scan(expert_step, start, (token_rows, cotan_rows, gate_weight, up_weight, down_weight, slot_token, slot_pick, slot_weight))
    return grad_sum, gate_sum.reshape(TOKENS, TOP)
```

```python
import functools

import jax
import jax.numpy as jnp
from jax import lax
from jax.experimental import pallas as pl
from jax.experimental.pallas import tpu as pltpu
from jax.sharding import PartitionSpec as P

BF = jnp.bfloat16
F32 = jnp.float32
PLANE = 8
LANES = 128


def dot(a, b):
    return jnp.dot(a, b, preferred_element_type=F32)


def dot_t(a, b):
    return lax.dot_general(a, b, (((1,), (1,)), ((), ())), preferred_element_type=F32)


def split_two(value):
    high = lax.reduce_precision(value, 8, 7)
    return high.astype(BF), (value - high).astype(BF)


def flipped(value, bits):
    result, weight = value * 0, 1
    while weight <= bits:
        digit = lax.rem(lax.div(value, weight), 2)
        result = result + weight * ((1 - digit) if bits & weight else digit)
        weight *= 2
    return result + weight * lax.div(value, weight)


def line_edges(planes):
    edges = []
    for k in range(planes):
        b = 1
        while b < planes and (k == 0 or b < (k & -k)):
            edges.append((k, b))
            b *= 2
    return edges


def remote(source, target, send_sem, recv_sem, other):
    return pltpu.make_async_remote_copy(
        src_ref=source,
        dst_ref=target,
        send_sem=send_sem,
        recv_sem=recv_sem,
        device_id={"ep": other},
        device_id_type=pl.DeviceIdType.MESH,
    )


def greet(partners):
    barrier = pltpu.get_barrier_semaphore()
    for other in partners:
        pl.semaphore_signal(
            barrier, inc=1, device_id={"ep": other}, device_id_type=pl.DeviceIdType.MESH
        )
    pl.semaphore_wait(barrier, len(partners))


def slot_numbers(shape, axis, cap, planes):
    number = lax.broadcasted_iota(jnp.int32, shape, axis).astype(F32)
    block = jnp.floor((number + 0.5) * (1.0 / cap))
    expert = jnp.floor((block + 0.5) * (1.0 / planes))
    return expert, block - expert * planes, number - block * cap


def dispatch_kernel(
    planes, cap, ahead, lag, ring,
    tokens_ref, cotangent_ref, aux_ref, gate_hbm, up_hbm, down_hbm,
    deltas_ref, gates_ref, every_aux_ref,
    zbuf, zaux, choose, packed, xbuf, gate_acc, up_acc, down_acc, gate_w, up_w, down_w,
    load_sem, own_sem, zsend_sem, zrecv_sem, asend_sem, arecv_sem, psend_sem, precv_sem,
    keep_sem,
):
    me = lax.axis_index("ep")
    z, r = lax.div(me, PLANE), lax.rem(me, PLANE)
    steps, _, tok, cw = zbuf.shape
    half = steps // 2
    owned, ff = gate_w.shape[0], gate_w.shape[2]
    lanes = choose.shape[1] // planes * 0 + LANES
    group = planes * cap
    slots = choose.shape[0]
    edges = line_edges(planes)

    def at(k, bits):
        return flipped(z, k) * PLANE + flipped(r, bits)

    loads = []
    for i, (source, target) in enumerate(
        ((gate_hbm, gate_w), (up_hbm, up_w), (down_hbm, down_w))
    ):
        loads.append(pltpu.make_async_copy(source, target, load_sem.at[i]))

    own_aux = pltpu.make_async_copy(aux_ref, zaux.at[z], keep_sem.at[steps])
    own_aux.start()
    for c in range(steps):
        source = tokens_ref if c < half else cotangent_ref
        columns = pl.ds((c % half) * cw, cw)
        pltpu.make_async_copy(source.at[:, columns], zbuf.at[c, z], own_sem.at[c]).start()
    for load in loads:
        load.start()

    greet([at(b, 0) for k, b in edges if k == 0] + [at(0, b) for b in range(1, PLANE)])

    def aux_hop(i):
        k, b = edges[i]
        slot = flipped(z, k)
        return remote(
            zaux.at[slot], zaux.at[slot], asend_sem.at[i], arecv_sem.at[slot], at(b, 0)
        )

    def aux_arrived(k):
        slot = flipped(z, k)
        remote(
            zaux.at[slot], zaux.at[slot], asend_sem.at[0], arecv_sem.at[slot], at(1, 0)
        ).wait_recv()

    def hop(c, i):
        k, b = edges[i]
        slot = flipped(z, k)
        return remote(
            zbuf.at[c, slot], zbuf.at[c, slot], zsend_sem.at[c, i], zrecv_sem.at[c, slot], at(b, 0)
        )

    def arrived(c, k):
        slot = flipped(z, k)
        remote(
            zbuf.at[c, slot], zbuf.at[c, slot], zsend_sem.at[c, 0], zrecv_sem.at[c, slot], at(1, 0)
        ).wait_recv()

    forwarded = [k for k in range(1, planes) if any(e[0] == k for e in edges)]
    plain = [k for k in range(1, planes) if k not in forwarded]

    def start_own(c):
        pltpu.make_async_copy(zbuf.at[c, z], zbuf.at[c, z], own_sem.at[c]).wait()
        for i, (k, b) in enumerate(edges):
            if k == 0:
                hop(c, i).start()

    def forward(c):
        for wanted in sorted(forwarded, reverse=True):
            arrived(c, wanted)
            for i, (k, b) in enumerate(edges):
                if k == wanted:
                    hop(c, i).start()

    own_aux.wait()
    for i, (k, b) in enumerate(edges):
        if k == 0:
            aux_hop(i).start()
    for c in range(ahead):
        start_own(c)
    for acc in (gate_acc, up_acc, down_acc):
        acc[...] = jnp.zeros(acc.shape, F32)
    for wanted in sorted(forwarded, reverse=True):
        aux_arrived(wanted)
        for i, (k, b) in enumerate(edges):
            if k == wanted:
                aux_hop(i).start()
    for k in plain:
        aux_arrived(k)
    forward(0)

    part = owned * group
    token = lax.broadcasted_iota(jnp.int32, (part, planes * tok), 1).astype(F32)
    token_z = jnp.floor((token + 0.5) * (1.0 / tok))
    _, slot_z, place = slot_numbers((part, planes * tok), 0, cap, planes)
    same_z = token_z == slot_z
    ranks = zaux[:, :, :LANES].reshape(planes * tok, LANES)
    lane = lax.broadcasted_iota(jnp.int32, (part, LANES), 1)
    expert = slot_numbers((part, LANES), 0, cap, planes)[0].astype(jnp.int32)

    @pl.loop(0, PLANE)
    def _(p):
        first = (z * PLANE + p) * owned
        spread = jnp.where(lane == expert + first, 1.0, 0.0).astype(BF)
        rank_of = dot_t(spread, ranks)
        rows = pl.ds(pl.multiple_of(p * part, 16), part)
        choose[rows, :] = jnp.where(same_z & (rank_of == place), 1.0, 0.0).astype(BF)

    def give(c, b):
        other = flipped(r, b)
        slot = lax.rem(c, ring)
        return remote(
            packed.at[slot, other], xbuf.at[c, r], psend_sem.at[slot, other], precv_sem.at[c, r],
            at(0, b),
        )

    def keep(c):
        return pltpu.make_async_copy(
            packed.at[lax.rem(c, ring), r], xbuf.at[c, r], keep_sem.at[c]
        )

    def pack(c):
        for k in plain:
            arrived(c, k)

        @pl.when(c >= ring)
        def _():
            for b in range(1, PLANE):
                give(c - ring, b).wait_send()

        block = zbuf[c].reshape(planes * tok, cw)
        picked = dot(choose[...], block).astype(BF)
        packed[lax.rem(c, ring)] = picked.reshape(PLANE, part, cw)
        for b in range(1, PLANE):
            give(c, b).start()
        keep(c).start()

    def compute(c):
        keep(c).wait()
        for b in range(1, PLANE):
            other = flipped(r, b)
            remote(
                xbuf.at[c, other], xbuf.at[c, other], psend_sem.at[0, 0], precv_sem.at[c, other],
                at(0, 1),
            ).wait_recv()
        rows = [
            xbuf[c, :, j * group:(j + 1) * group, :].reshape(PLANE * group, cw)
            for j in range(owned)
        ]

        @pl.when(c < half)
        def _():
            depth = pl.ds(pl.multiple_of(c * cw, cw), cw)
            for j in range(owned):
                gate_acc[j] += dot(rows[j], gate_w[j, depth, :])
                up_acc[j] += dot(rows[j], up_w[j, depth, :])

        @pl.when(c >= half)
        def _():
            depth = pl.ds(pl.multiple_of((c - half) * cw, cw), cw)
            for j in range(owned):
                down_acc[j] += dot_t(rows[j], down_w[j, :, depth])

    for load in loads:
        load.wait()

    @pl.loop(0, steps + lag)
    def _(c):
        @pl.when(c + ahead < steps)
        def _():
            start_own(c + ahead)

        @pl.when(c + 1 < steps)
        def _():
            forward(c + 1)

        @pl.when(c < steps)
        def _():
            pack(c)

        @pl.when(c >= lag)
        def _():
            compute(c - lag)

    column = lax.broadcasted_iota(jnp.int32, (group, LANES), 1)

    @pl.loop(0, PLANE)
    def _(p):
        rows = pl.ds(pl.multiple_of(p * group, 16), group)
        for j in range(owned):
            gate_pre, up_pre, upward = gate_acc[j, rows, :], up_acc[j, rows, :], down_acc[j, rows, :]
            sigma = 1.0 / (1.0 + jnp.exp(-gate_pre))
            silu_val = gate_pre * sigma
            up_delta = upward * silu_val
            pick_gate = jnp.sum(up_delta * up_pre, axis=1, keepdims=True)
            gate_delta = upward * up_pre * sigma * (1.0 + gate_pre * (1.0 - sigma))
            deltas_ref[j, rows, :ff] = gate_delta.astype(BF)
            deltas_ref[j, rows, ff:] = up_delta.astype(BF)
            high = pick_gate.astype(BF).astype(F32)
            low = pick_gate - high
            both = jnp.where(column == 0, high, jnp.where(column == 1, low, 0.0))
            gates_ref[j, rows, :] = both.astype(BF)

    every_aux_ref[...] = zaux[...]

    for i in range(len(edges)):
        aux_hop(i).wait_send()

    @pl.loop(0, steps)
    def _(c):
        for i in range(len(edges)):
            hop(c, i).wait_send()

    @pl.loop(steps - ring, steps)
    def _(c):
        for b in range(1, PLANE):
            give(c, b).wait_send()


def dispatch(planes, cap, tokens, cotangent, aux, gate_weight, up_weight, down_weight):
    tok, width = tokens.shape
    owned, _, ff = gate_weight.shape
    cw = min(512, width)
    steps = 2 * width // cw
    ring = min(4, steps)
    group = planes * cap
    part, rows = owned * group, PLANE * group
    edges = len(line_edges(planes))
    vmem = pl.BlockSpec(memory_space=pltpu.VMEM)
    hbm = pl.BlockSpec(memory_space=pl.ANY)
    dma = pltpu.SemaphoreType.DMA
    return pl.pallas_call(
        functools.partial(dispatch_kernel, planes, cap, min(2, steps), 2, ring),
        out_shape=(
            jax.ShapeDtypeStruct((owned, rows, 2 * ff), BF),
            jax.ShapeDtypeStruct((owned, rows, LANES), BF),
            jax.ShapeDtypeStruct((planes,) + aux.shape, BF),
        ),
        in_specs=[hbm, hbm, vmem, hbm, hbm, hbm],
        out_specs=(vmem, vmem, vmem),
        scratch_shapes=[
            pltpu.VMEM((steps, planes, tok, cw), BF),
            pltpu.VMEM((planes,) + aux.shape, BF),
            pltpu.VMEM((PLANE * part, planes * tok), BF),
            pltpu.VMEM((ring, PLANE, part, cw), BF),
            pltpu.VMEM((steps, PLANE, part, cw), BF),
            pltpu.VMEM((owned, rows, ff), F32),
            pltpu.VMEM((owned, rows, ff), F32),
            pltpu.VMEM((owned, rows, ff), F32),
            pltpu.VMEM(gate_weight.shape, BF),
            pltpu.VMEM(up_weight.shape, BF),
            pltpu.VMEM(down_weight.shape, BF),
            dma((3,)),
            dma((steps,)),
            dma((steps, edges)),
            dma((steps, planes)),
            dma((edges,)),
            dma((planes,)),
            dma((ring, PLANE)),
            dma((steps, PLANE)),
            dma((steps + 1,)),
        ],
        compiler_params=pltpu.CompilerParams(
            collective_id=0, has_side_effects=True, vmem_limit_bytes=63 * 2**20
        ),
    )(tokens, cotangent, aux, gate_weight, up_weight, down_weight)


def combine_kernel(
    planes, cap,
    deltas_ref, gates_ref, aux_ref, gate_hbm, up_hbm,
    out_ref, gate_out,
    gate_w, up_w, rsend, rrecv, gsend, grecv, marks, mix_high, mix_low, zsend, zrecv,
    zgsend, zgrecv,
    load_sem, rsend_sem, rrecv_sem, gsend_sem, grecv_sem, zsend_sem, zrecv_sem,
    zgsend_sem, zgrecv_sem,
):
    me = lax.axis_index("ep")
    z, r = lax.div(me, PLANE), lax.rem(me, PLANE)
    steps, _, part, cw = rsend.shape
    tok = out_ref.shape[0]
    owned, ff = gate_w.shape[0], gate_w.shape[2]
    group = planes * cap
    slots = PLANE * part

    def at(k, bits):
        return flipped(z, k) * PLANE + flipped(r, bits)

    loads = []
    for i, (source, target) in enumerate(((gate_hbm, gate_w), (up_hbm, up_w))):
        loads.append(pltpu.make_async_copy(source, target, load_sem.at[i]))
        loads[-1].start()

    for j in range(owned):
        gsend[:, j * group:(j + 1) * group, :] = gates_ref[j].reshape(PLANE, group, LANES)
    greet([at(k, 0) for k in range(1, planes)] + [at(0, b) for b in range(1, PLANE)])

    def give(c, b):
        return remote(
            rsend.at[c, flipped(r, b)], rrecv.at[c, r], rsend_sem.at[c, b], rrecv_sem.at[c, r],
            at(0, b),
        )

    def keep(c):
        return pltpu.make_async_copy(rsend.at[c, r], rrecv.at[c, r], rsend_sem.at[c, 0])

    def give_gate(b):
        return remote(
            gsend.at[flipped(r, b)], grecv.at[r], gsend_sem.at[b], grecv_sem.at[r], at(0, b)
        )

    keep_gate = pltpu.make_async_copy(gsend.at[r], grecv.at[r], gsend_sem.at[0])

    def home(c, k):
        slot = flipped(z, k)
        return remote(
            zsend.at[c, slot], zrecv.at[c, z], zsend_sem.at[c, k], zrecv_sem.at[c, z], at(k, 0)
        )

    def home_gate(k):
        slot = flipped(z, k)
        return remote(
            zgsend.at[slot], zgrecv.at[z], zgsend_sem.at[k], zgrecv_sem.at[z], at(k, 0)
        )

    for load in loads:
        load.wait()

    @pl.loop(0, steps)
    def _(c):
        depth = pl.ds(pl.multiple_of(c * cw, cw), cw)
        for j in range(owned):
            back = dot_t(deltas_ref[j, :, :ff], gate_w[j, depth, :])
            back = back + dot_t(deltas_ref[j, :, ff:], up_w[j, depth, :])
            rsend[c, :, j * group:(j + 1) * group, :] = back.astype(BF).reshape(PLANE, group, cw)
        for b in range(1, PLANE):
            give(c, b).start()
        keep(c).start()

    for b in range(1, PLANE):
        give_gate(b).start()
    keep_gate.start()

    token = lax.broadcasted_iota(jnp.int32, (tok, part), 1)
    expert_of, slot_z, place = slot_numbers((tok, part), 1, cap, planes)
    lane = lax.broadcasted_iota(jnp.int32, (part, LANES), 1)
    expert = slot_numbers((part, LANES), 0, cap, planes)[0].astype(jnp.int32)

    for p in range(PLANE):
        first = (z * PLANE + p) * owned
        spread = jnp.where(lane == expert + first, 1.0, 0.0).astype(BF)
        columns = slice(p * part, (p + 1) * part)
        for k in range(planes):
            rows = slice(k * tok, (k + 1) * tok)
            values = aux_ref[k]
            rank_of = dot_t(values[:, :LANES], spread)
            hit = (rank_of == place) & (slot_z == float(k))
            marks[rows, columns] = jnp.where(hit, 1.0, 0.0).astype(BF)
            high = dot_t(values[:, LANES:2 * LANES], spread)
            low = dot_t(values[:, 2 * LANES:], spread)
            mix_high[rows, columns] = jnp.where(hit, high, 0.0).astype(BF)
            mix_low[rows, columns] = jnp.where(hit, low, 0.0).astype(BF)

    @pl.loop(0, steps)
    def _(c):
        keep(c).wait()
        for b in range(1, PLANE):
            other = flipped(r, b)
            remote(
                rrecv.at[c, other], rrecv.at[c, other], rsend_sem.at[c, 0],
                rrecv_sem.at[c, other], at(0, 1),
            ).wait_recv()
        rows = rrecv[c].reshape(slots, cw)
        total = dot(mix_high[...], rows) + dot(mix_low[...], rows)
        zsend[c] = total.astype(BF).reshape(planes, tok, cw)
        for k in range(1, planes):
            home(c, k).start()
        own = pl.ds(pl.multiple_of(z * tok, tok), tok)
        columns = pl.ds(pl.multiple_of(c * cw, cw), cw)
        mine = dot(mix_high[own, :], rows) + dot(mix_low[own, :], rows)
        out_ref[:, columns] = mine

    keep_gate.wait()
    for b in range(1, PLANE):
        other = flipped(r, b)
        remote(
            grecv.at[other], grecv.at[other], gsend_sem.at[0], grecv_sem.at[other], at(0, 1)
        ).wait_recv()
    picked = grecv[...].reshape(slots, LANES)
    lane_of = lax.broadcasted_iota(jnp.int32, (slots, LANES), 1)
    own_expert = slot_numbers((slots, LANES), 0, cap, planes)[0].astype(jnp.int32)
    here = lane_of == own_expert + z * PLANE * owned
    zero = jnp.zeros((), F32)
    column = lax.broadcasted_iota(jnp.int32, (slots, LANES), 1)
    high = jnp.sum(jnp.where(column == 0, picked.astype(F32), zero), axis=1, keepdims=True)
    low = jnp.sum(jnp.where(column == 1, picked.astype(F32), zero), axis=1, keepdims=True)
    high = jnp.where(here, high, zero).astype(BF)
    low = jnp.where(here, low, zero).astype(BF)
    gates = dot(marks[...], high) + dot(marks[...], low)
    zgsend[...] = gates.reshape(planes, tok, LANES)
    for k in range(1, planes):
        home_gate(k).start()
    gate_out[...] = zgsend[z]

    @pl.loop(0, steps)
    def _(c):
        columns = pl.ds(pl.multiple_of(c * cw, cw), cw)
        total = out_ref[:, columns]
        for k in range(1, planes):
            slot = flipped(z, k)
            remote(
                zrecv.at[c, slot], zrecv.at[c, slot], zsend_sem.at[c, 0], zrecv_sem.at[c, slot],
                at(1, 0),
            ).wait_recv()
            total = total + zrecv[c, slot].astype(F32)
        out_ref[:, columns] = total

    total = gate_out[...]
    for k in range(1, planes):
        slot = flipped(z, k)
        remote(
            zgrecv.at[slot], zgrecv.at[slot], zgsend_sem.at[0], zgrecv_sem.at[slot], at(1, 0)
        ).wait_recv()
        total = total + zgrecv[slot]
    gate_out[...] = total

    @pl.loop(0, steps)
    def _(c):
        for b in range(1, PLANE):
            give(c, b).wait_send()
        for k in range(1, planes):
            home(c, k).wait_send()

    for b in range(1, PLANE):
        give_gate(b).wait_send()
    for k in range(1, planes):
        home_gate(k).wait_send()


def combine(planes, cap, tok, deltas, gates, every_aux, gate_weight, up_weight):
    owned, width, ff = gate_weight.shape
    cw = min(512, width)
    steps = width // cw
    part = owned * planes * cap
    slots = PLANE * part
    vmem = pl.BlockSpec(memory_space=pltpu.VMEM)
    hbm = pl.BlockSpec(memory_space=pl.ANY)
    dma = pltpu.SemaphoreType.DMA
    return pl.pallas_call(
        functools.partial(combine_kernel, planes, cap),
        out_shape=(
            jax.ShapeDtypeStruct((tok, width), F32),
            jax.ShapeDtypeStruct((tok, LANES), F32),
        ),
        in_specs=[vmem, vmem, vmem, hbm, hbm],
        out_specs=(vmem, vmem),
        scratch_shapes=[
            pltpu.VMEM(gate_weight.shape, BF),
            pltpu.VMEM(up_weight.shape, BF),
            pltpu.VMEM((steps, PLANE, part, cw), BF),
            pltpu.VMEM((steps, PLANE, part, cw), BF),
            pltpu.VMEM((PLANE, part, LANES), BF),
            pltpu.VMEM((PLANE, part, LANES), BF),
            pltpu.VMEM((planes * tok, slots), BF),
            pltpu.VMEM((planes * tok, slots), BF),
            pltpu.VMEM((planes * tok, slots), BF),
            pltpu.VMEM((steps, planes, tok, cw), BF),
            pltpu.VMEM((steps, planes, tok, cw), BF),
            pltpu.VMEM((planes, tok, LANES), F32),
            pltpu.VMEM((planes, tok, LANES), F32),
            dma((2,)),
            dma((steps, PLANE)),
            dma((steps, PLANE)),
            dma((PLANE,)),
            dma((PLANE,)),
            dma((steps, planes)),
            dma((steps, planes)),
            dma((planes,)),
            dma((planes,)),
        ],
        compiler_params=pltpu.CompilerParams(
            collective_id=1, has_side_effects=True, vmem_limit_bytes=60 * 2**20
        ),
    )(deltas, gates, every_aux, gate_weight, up_weight)


def by_planes(planes, tokens, cotangent, routing, expert_ids, gate_weight, up_weight, down_weight):
    owned = gate_weight.shape[0]
    experts = owned * planes * PLANE
    tok, top = expert_ids.shape
    cap = 5 * tok * top // (4 * experts)
    onehot = expert_ids[:, :, None] == jnp.arange(LANES, dtype=jnp.int32)[None, None, :]
    picked = jnp.any(onehot, axis=1)
    row = jnp.arange(tok, dtype=jnp.int32)
    lower = (row[:, None] > row[None, :]).astype(BF)
    rank = jnp.where(picked, dot(lower, picked.astype(BF)), -1.0).astype(BF)
    amount = jnp.sum(jnp.where(onehot, routing[:, :, None], 0.0), axis=1)
    amount_high, amount_low = split_two(amount)
    aux = jnp.concatenate([rank, amount_high, amount_low], axis=1)
    deltas, gates, every_aux = dispatch(
        planes, cap, tokens, cotangent, aux, gate_weight, up_weight, down_weight
    )
    input_grad, gate_sum = combine(
        planes, cap, tok, deltas, gates, every_aux, gate_weight, up_weight
    )
    gate_grad = jnp.sum(jnp.where(onehot, gate_sum[:, None, :], 0.0), axis=2)
    return input_grad, gate_grad


def local(tokens, cotangent, routing, expert_ids, gate_weight, up_weight, down_weight):
    count = lax.axis_size("ep")
    owned = gate_weight.shape[0]
    experts = owned * count
    tok_rows, top = expert_ids.shape
    width = tokens.shape[1]
    cap = 5 * tok_rows * top // (4 * experts)
    slots = experts * cap

    onehot = expert_ids[:, :, None] == jnp.arange(experts, dtype=jnp.int32)[None, None, :]
    picked = jnp.any(onehot, axis=1)
    row = jnp.arange(tok_rows, dtype=jnp.int32)
    lower = (row[:, None] > row[None, :]).astype(BF)
    before = dot(lower, picked.astype(BF))
    rank = jnp.where(picked, before, -1.0).astype(BF)
    slot = jnp.arange(slots, dtype=jnp.int32)
    spread = (slot[:, None] // cap == jnp.arange(experts, dtype=jnp.int32)[None, :]).astype(BF)
    place = (slot % cap).astype(F32)
    rank_of = lax.dot_general(spread, rank, (((1,), (1,)), ((), ())), preferred_element_type=F32)
    choose = (rank_of == place[:, None]).astype(BF)
    rank_back = lax.dot_general(rank, spread, (((1,), (1,)), ((), ())), preferred_element_type=F32)
    choose_back = rank_back == place[None, :]

    def exchange(value):
        return lax.all_to_all(value, "ep", split_axis=0, concat_axis=0, tiled=True)

    def by_expert(value):
        value = value.reshape(count, owned, cap, value.shape[1])
        return value.transpose(1, 0, 2, 3).reshape(owned, count * cap, value.shape[3])

    def by_source(value):
        value = value.reshape(owned, count, cap, value.shape[2])
        return value.transpose(1, 0, 2, 3).reshape(slots, value.shape[3])

    inputs = by_expert(exchange(dot(choose, tokens).astype(BF)))
    grads_in = by_expert(exchange(dot(choose, cotangent).astype(BF)))
    gate_pre = jnp.einsum("erd,edf->erf", inputs, gate_weight, preferred_element_type=F32)
    up_pre = jnp.einsum("erd,edf->erf", inputs, up_weight, preferred_element_type=F32)
    upward = jnp.einsum("erd,efd->erf", grads_in, down_weight, preferred_element_type=F32)
    sigma = jax.nn.sigmoid(gate_pre)
    silu_val = gate_pre * sigma
    pick_gate = jnp.sum(silu_val * up_pre * upward, axis=2, keepdims=True)
    gate_delta = (upward * up_pre * sigma * (1.0 + gate_pre * (1.0 - sigma))).astype(BF)
    up_delta = (upward * silu_val).astype(BF)
    deltas = jnp.concatenate([gate_delta, up_delta], axis=2)
    joined = jnp.concatenate([gate_weight, up_weight], axis=2)

    half = width // 2
    gate_high, gate_low = split_two(pick_gate)
    lane = jnp.arange(128, dtype=jnp.int32)[None, None, :]
    gate_cols = jnp.where(lane == 0, gate_high, jnp.where(lane == 1, gate_low, jnp.zeros((), BF)))
    first = jnp.einsum("erf,edf->erd", deltas, joined[:, :half], preferred_element_type=F32).astype(BF)
    second = jnp.einsum("erf,edf->erd", deltas, joined[:, half:], preferred_element_type=F32).astype(BF)
    back_a = exchange(by_source(jnp.concatenate([first, gate_cols], axis=2)))
    back_b = exchange(by_source(second))

    amount = jnp.sum(jnp.where(onehot, routing[:, :, None], 0.0), axis=1)
    amount_high, amount_low = split_two(amount)
    zero = jnp.zeros((), BF)

    def mix(part):
        wide = lax.dot_general(part, spread, (((1,), (1,)), ((), ())), preferred_element_type=F32)
        return jnp.where(choose_back, wide.astype(BF), zero)

    mixing = jnp.concatenate([mix(amount_high), mix(amount_low)], axis=0)

    def combine(value):
        both = dot(mixing, value)
        return both[:tok_rows] + both[tok_rows:]

    weighted = jnp.concatenate([combine(back_a[:, :half]), combine(back_b)], axis=1)
    gates = back_a[:, half:half + 2].T

    def gate_part(i):
        return dot(jnp.where(choose_back, gates[i][None, :], zero), spread)

    gate_sum = gate_part(0) + gate_part(1)
    gate_grad = jnp.sum(jnp.where(onehot, gate_sum[:, None, :], 0.0), axis=2)
    input_grad = lax.psum_scatter(weighted, "hid", scatter_dimension=1, tiled=True)
    return (input_grad, lax.psum(gate_grad, "hid"))


def solution(mesh):
    placed = (
        P(("rep", "ep"), None),
        P(("rep", "ep"), None),
        P(("rep", "ep"), None),
        P(("rep", "ep"), None),
        P("ep", None, "hid"),
        P("ep", None, "hid"),
        P("ep", "hid", None),
    )
    count = mesh.shape["ep"]
    planes = count // PLANE
    direct = (
        mesh.shape["rep"] * mesh.shape["hid"] == 1
        and count % PLANE == 0
        and planes > 1
        and planes & (planes - 1) == 0
    )

    def run(tokens, cotangent, routing, expert_ids, gate_weight, *rest):
        tok, top = expert_ids.shape
        owned, width, ff = gate_weight.shape
        cap = 5 * tok * top // (4 * owned * count)
        fits = (
            direct
            and owned * count <= LANES
            and planes * cap % 16 == 0
            and tok % 16 == 0
            and width % 512 == 0
            and ff % LANES == 0
        )
        body = functools.partial(by_planes, planes) if fits else local
        return body(tokens, cotangent, routing, expert_ids, gate_weight, *rest)

    return jax.shard_map(
        run,
        mesh=mesh,
        in_specs=placed,
        out_specs=(P(("rep", "ep"), "hid"), P(("rep", "ep"), None)),
        check_vma=False,
    )
```

```python
import functools

import jax
import jax.numpy as jnp
from jax import lax
from jax.experimental import pallas as pl
from jax.experimental.pallas import tpu as pltpu
from jax.sharding import PartitionSpec as P

BF = jnp.bfloat16
F32 = jnp.float32
PLANE = 8
LANES = 128
COLUMNS = 256


def dot(a, b):
    return jnp.dot(a, b, preferred_element_type=F32)


def dot_t(a, b):
    return lax.dot_general(a, b, (((1,), (1,)), ((), ())), preferred_element_type=F32)


def split_two(value):
    high = lax.reduce_precision(value, 8, 7)
    return high.astype(BF), (value - high).astype(BF)


def flipped(value, bits):
    result, weight = value * 0, 1
    while weight <= bits:
        digit = lax.rem(lax.div(value, weight), 2)
        result = result + weight * ((1 - digit) if bits & weight else digit)
        weight *= 2
    return result + weight * lax.div(value, weight)


def line_edges(planes):
    edges = []
    for k in range(planes):
        b = 1
        while b < planes and (k == 0 or b < (k & -k)):
            edges.append((k, b))
            b *= 2
    return edges


def remote(source, target, send_sem, recv_sem, other):
    return pltpu.make_async_remote_copy(
        src_ref=source,
        dst_ref=target,
        send_sem=send_sem,
        recv_sem=recv_sem,
        device_id={"ep": other},
        device_id_type=pl.DeviceIdType.MESH,
    )


def greet(partners):
    barrier = pltpu.get_barrier_semaphore()
    for other in partners:
        pl.semaphore_signal(
            barrier, inc=1, device_id={"ep": other}, device_id_type=pl.DeviceIdType.MESH
        )
    pl.semaphore_wait(barrier, len(partners))


def slot_numbers(shape, axis, cap, planes):
    number = lax.broadcasted_iota(jnp.int32, shape, axis).astype(F32)
    block = jnp.floor((number + 0.5) * (1.0 / cap))
    expert = jnp.floor((block + 0.5) * (1.0 / planes))
    return expert, block - expert * planes, number - block * cap


def fused_kernel(
    planes, cap, ring, lag,
    tokens_ref, cotangent_ref, aux_ref, gate_hbm, up_hbm, down_hbm,
    out_ref, gate_out,
    zbuf, pbuf, zaux, paux, choose_line, choose_plane, reorder, packed_line, packed_plane,
    xline, xplane, gate_acc, up_acc, down_acc, gate_w, up_w, down_w,
    rrecv, gsend, grecv, marks, mix_high, mix_low, zsend, zrecv, zgsend, zgrecv,
    load_sem, own_sem, aux_sem, zas_sem, zar_sem, pas_sem, par_sem, zs_sem, zr_sem, ps_sem, pr_sem,
    ls_sem, lr_sem, bs_sem, br_sem, keep_sem, rs_sem, rr_sem, gs_sem, gr_sem, hs_sem, hr_sem,
    hgs_sem, hgr_sem,
):
    me = lax.axis_index("ep")
    z, r = lax.div(me, PLANE), lax.rem(me, PLANE)
    supers, _, tok, cw = pbuf.shape
    steps = 4 * supers
    half = steps // 2
    owned, ff = gate_w.shape[1], gate_w.shape[3]
    group = planes * cap
    part = owned * group
    wide = PLANE * cap
    part_plane = owned * wide
    slots = PLANE * part
    deltas = ff // cw
    edges = line_edges(planes)

    def at(k, bits):
        return flipped(z, k) * PLANE + flipped(r, bits)

    core = lax.rem(r, 2)
    along_x, along_y, across, twin = (flipped(r, b) for b in (2, 4, 6, 1))
    near = along_x + core * (along_y - along_x)
    then = along_y + core * (along_x - along_y)

    def line_index(s, i):
        return 3 * s + (0, None, 1, 2)[i]

    own_aux = pltpu.make_async_copy(aux_ref, zaux.at[z], aux_sem.at[0])
    own_ranks = pltpu.make_async_copy(aux_ref.at[:, :LANES], paux.at[r], aux_sem.at[1])
    own_aux.start()
    own_ranks.start()
    for q in range(steps):
        source = tokens_ref if q < half else cotangent_ref
        columns = pl.ds((q % half) * cw, cw)
        s, i = q // 4, q % 4
        target = pbuf.at[s, r] if i == 1 else zbuf.at[line_index(s, i), z]
        pltpu.make_async_copy(source.at[:, columns], target, own_sem.at[q]).start()

    def first_loads(n, slot):
        depth = pl.ds(pl.multiple_of(n * cw, cw), cw)
        return [
            pltpu.make_async_copy(w.at[:, depth, :], buf.at[slot], load_sem.at[k, slot])
            for k, (w, buf) in enumerate(((gate_hbm, gate_w), (up_hbm, up_w)))
        ]

    def down_load(n, slot):
        depth = pl.ds(pl.multiple_of((n - half) * cw, cw), cw)
        return pltpu.make_async_copy(
            down_hbm.at[:, :, depth], down_w.at[slot], load_sem.at[2, slot]
        )

    for load in first_loads(0, 0):
        load.start()

    greet([at(k, 0) for k in range(1, planes)] + [at(0, b) for b in range(1, PLANE)])

    def line_hop(buf, sems, rems, index, e):
        k, b = edges[e]
        slot = flipped(z, k)
        return remote(
            buf.at[index + (slot,)], buf.at[index + (slot,)], sems.at[index + (e,)],
            rems.at[index + (slot,)], at(b, 0),
        )

    def line_arrived(buf, sems, rems, index, k):
        slot = flipped(z, k)
        remote(
            buf.at[index + (slot,)], buf.at[index + (slot,)], sems.at[index + (0,)],
            rems.at[index + (slot,)], at(1, 0),
        ).wait_recv()

    forwarded = sorted({k for k, b in edges if k}, reverse=True)
    plain = [k for k in range(1, planes) if k not in forwarded]
    data, ranks_of = (zbuf, zs_sem, zr_sem), (zaux, zas_sem, zar_sem)

    def line_start(kind, index):
        for e, (k, b) in enumerate(edges):
            if k == 0:
                line_hop(*kind, index, e).start()

    def line_forward(kind, index):
        for wanted in forwarded:
            line_arrived(*kind, index, wanted)
            for e, (k, b) in enumerate(edges):
                if k == wanted:
                    line_hop(*kind, index, e).start()

    def line_rest(kind, index):
        for k in plain:
            line_arrived(*kind, index, k)

    def line_own(s, i):
        a = line_index(s, i)
        pltpu.make_async_copy(zbuf.at[a, z], zbuf.at[a, z], own_sem.at[4 * s + i]).wait()
        line_start(data, (a,))

    hops = [
        [(r, near, 0), (r, then, 1), (r, twin, 2)],
        [(near, then, 3), (near, twin, 4), (then, twin, 5)],
        [(across, twin, 6)],
    ]

    def plane_hop(s, hop):
        slot, other, e = hop
        return remote(
            pbuf.at[s, slot], pbuf.at[s, slot], ps_sem.at[s, e], pr_sem.at[s, slot],
            z * PLANE + other,
        )

    def plane_arrived(s, slot):
        remote(
            pbuf.at[s, slot], pbuf.at[s, slot], ps_sem.at[s, 0], pr_sem.at[s, slot], at(0, 1)
        ).wait_recv()

    def plane_stage(s, stage):
        if stage == 0:
            pltpu.make_async_copy(pbuf.at[s, r], pbuf.at[s, r], own_sem.at[4 * s + 1]).wait()
        elif stage == 1:
            plane_arrived(s, near)
            plane_arrived(s, then)
        elif stage == 2:
            plane_arrived(s, across)
        else:
            for b in (1, 3, 5, 7):
                plane_arrived(s, flipped(r, b))
            return
        for hop in hops[stage]:
            plane_hop(s, hop).start()

    def ranks_hop(b):
        return remote(
            paux.at[r], paux.at[r], pas_sem.at[b], par_sem.at[r], at(0, b)
        )

    own_aux.wait()
    line_start(ranks_of, ())
    line_own(0, 0)
    own_ranks.wait()
    for b in range(1, PLANE):
        ranks_hop(b).start()
    plane_stage(0, 0)
    line_own(0, 2)

    token = lax.broadcasted_iota(jnp.int32, (part, planes * tok), 1).astype(F32)
    token_z = jnp.floor((token + 0.5) * (1.0 / tok))
    _, slot_z, place = slot_numbers((part, planes * tok), 0, cap, planes)
    same_z = token_z == slot_z
    lane = lax.broadcasted_iota(jnp.int32, (part, LANES), 1)
    expert = slot_numbers((part, LANES), 0, cap, planes)[0].astype(jnp.int32)
    line_forward(ranks_of, ())
    line_rest(ranks_of, ())
    line_forward(data, (0,))
    line_forward(data, (1,))
    ranks = zaux[:, :, :LANES].reshape(planes * tok, LANES)

    @pl.loop(0, PLANE)
    def _(p):
        first = (z * PLANE + p) * owned
        spread = jnp.where(lane == expert + first, 1.0, 0.0).astype(BF)
        rank_of = dot_t(spread, ranks)
        rows = pl.ds(pl.multiple_of(p * part, 16), part)
        choose_line[rows, :] = jnp.where(same_z & (rank_of == place), 1.0, 0.0).astype(BF)

    def choose_in_plane():
        for b in range(1, PLANE):
            other = flipped(r, b)
            remote(
                paux.at[other], paux.at[other], pas_sem.at[0], par_sem.at[other], at(0, 1)
            ).wait_recv()
        token = lax.broadcasted_iota(jnp.int32, (part_plane, PLANE * tok), 1).astype(F32)
        token_from = jnp.floor((token + 0.5) * (1.0 / tok))
        _, slot_from, place = slot_numbers((part_plane, PLANE * tok), 0, cap, PLANE)
        same = token_from == slot_from
        lane = lax.broadcasted_iota(jnp.int32, (part_plane, LANES), 1)
        expert = slot_numbers((part_plane, LANES), 0, cap, PLANE)[0].astype(jnp.int32)
        ranks = paux[...].reshape(PLANE * tok, LANES)

        @pl.loop(0, planes)
        def _(k):
            first = (k * PLANE + r) * owned
            spread = jnp.where(lane == expert + first, 1.0, 0.0).astype(BF)
            rank_of = dot_t(spread, ranks)
            rows = pl.ds(pl.multiple_of(k * part_plane, 16), part_plane)
            choose_plane[rows, :] = jnp.where(same & (rank_of == place), 1.0, 0.0).astype(BF)

        size = PLANE * group
        _, from_z, place = slot_numbers((size, size), 0, cap, planes)
        origin = slot_numbers((size, size), 0, cap, planes)[0]
        column = lax.broadcasted_iota(jnp.int32, (size, size), 1).astype(F32)
        wanted = (from_z * PLANE + origin) * cap + place
        reorder[...] = jnp.where(column == wanted, 1.0, 0.0).astype(BF)

    def line_give(a, b):
        other = flipped(r, b)
        slot = lax.rem(a, ring)
        return remote(
            packed_line.at[slot, other], xline.at[a, r], ls_sem.at[slot, other], lr_sem.at[a, r],
            at(0, b),
        )

    def line_keep(a):
        return pltpu.make_async_copy(
            packed_line.at[lax.rem(a, ring), r], xline.at[a, r], keep_sem.at[a]
        )

    def pack_line(a):
        line_rest(data, (a,))

        @pl.when(a >= ring)
        def _():
            for b in range(1, PLANE):
                line_give(a - ring, b).wait_send()

        picked = dot(choose_line[...], zbuf[a].reshape(planes * tok, cw)).astype(BF)
        packed_line[lax.rem(a, ring)] = picked.reshape(PLANE, part, cw)
        for b in (6, 7, 2, 4, 3, 5, 1):
            line_give(a, b).start()
        line_keep(a).start()

    def plane_give(s, k):
        other = flipped(z, k)
        return remote(
            packed_plane.at[s, other], xplane.at[s, z], bs_sem.at[s, k], br_sem.at[s, z], at(k, 0)
        )

    def plane_keep(s):
        return pltpu.make_async_copy(packed_plane.at[s, z], xplane.at[s, z], bs_sem.at[s, 0])

    def pack_plane(s):
        picked = dot(choose_plane[...], pbuf[s].reshape(PLANE * tok, cw)).astype(BF)
        packed_plane[s] = picked.reshape(planes, part_plane, cw)
        for k in range(planes - 1, 0, -1):
            plane_give(s, k).start()
        plane_keep(s).start()

    def rows_line(a):
        line_keep(a).wait()
        for b in range(1, PLANE):
            other = flipped(r, b)
            remote(
                xline.at[a, other], xline.at[a, other], ls_sem.at[0, 0], lr_sem.at[a, other],
                at(0, 1),
            ).wait_recv()
        return [
            xline[a, :, j * group:(j + 1) * group, :].reshape(PLANE * group, cw)
            for j in range(owned)
        ]

    def rows_plane(s):
        plane_keep(s).wait()
        for k in range(1, planes):
            other = flipped(z, k)
            remote(
                xplane.at[s, other], xplane.at[s, other], bs_sem.at[s, 0], br_sem.at[s, other],
                at(1, 0),
            ).wait_recv()
        return [
            dot(
                reorder[...],
                xplane[s, :, j * wide:(j + 1) * wide, :].reshape(PLANE * group, cw),
            ).astype(BF)
            for j in range(owned)
        ]

    def compute(s, i):
        n = 4 * s + i
        slot = i % 2
        rows = rows_plane(s) if i == 1 else rows_line(line_index(s, i))

        @pl.when(n + 1 < half)
        def _():
            for load in first_loads(n + 1, 1 - slot):
                load.start()

        @pl.when((n + 1 >= half) & (n + 1 < steps))
        def _():
            down_load(n + 1, 1 - slot).start()

        @pl.when(n + 1 == steps)
        def _():
            for load in first_loads(0, 1 - slot):
                load.start()

        @pl.when(n < half)
        def _():
            for load in first_loads(n, slot):
                load.wait()
            for j in range(owned):
                gate_acc[j] += dot(rows[j], gate_w[slot, j])
                up_acc[j] += dot(rows[j], up_w[slot, j])

        @pl.when(n >= half)
        def _():
            down_load(n, slot).wait()
            for j in range(owned):
                down_acc[j] += dot_t(rows[j], down_w[slot, j])

    def mix(p):
        _, slot_z, place = slot_numbers((tok, part), 1, cap, planes)
        first = (z * PLANE + p) * owned
        spread = jnp.where(lane == expert + first, 1.0, 0.0).astype(BF)
        columns = slice(p * part, (p + 1) * part)
        for k in range(planes):
            rows = slice(k * tok, (k + 1) * tok)
            values = zaux[k]
            rank_of = dot_t(values[:, :LANES], spread)
            hit = (rank_of == place) & (slot_z == float(k))
            marks[rows, columns] = jnp.where(hit, 1.0, 0.0).astype(BF)
            high = dot_t(values[:, LANES:2 * LANES], spread)
            low = dot_t(values[:, 2 * LANES:], spread)
            mix_high[rows, columns] = jnp.where(hit, high, 0.0).astype(BF)
            mix_low[rows, columns] = jnp.where(hit, low, 0.0).astype(BF)

    @pl.loop(0, supers + 2)
    def _(s):
        for i in range(4):
            @pl.when(s < supers)
            def _():
                if i == 1:
                    @pl.when(s == 0)
                    def _():
                        choose_in_plane()

                    plane_stage(s, 3)
                    pack_plane(s)
                else:
                    early = {0: ((0, 3), (1, 0)), 2: ((1, 2), (1, 3)), 3: ((2, 0),)}[i]
                    later = {0: (s + 1, 3), 2: (s + 2, 0), 3: (s + 2, 2)}[i]
                    follow = {0: (s, 3), 2: (s + 1, 0), 3: (s + 1, 2)}[i]

                    @pl.when(s == 0)
                    def _():
                        for item in early:
                            if item[0] < supers:
                                line_own(*item)

                    if i == 3:
                        @pl.when(s == 0)
                        def _():
                            if 2 < supers:
                                line_own(2, 2)

                    @pl.when((s >= 1) & (later[0] < supers))
                    def _():
                        line_own(*later)

                    pack_line(line_index(s, i))

                    @pl.when(follow[0] < supers)
                    def _():
                        line_forward(data, (line_index(*follow),))
                if i == 0:
                    @pl.when(s == 0)
                    def _():
                        for stage in (1, 2):
                            plane_stage(0, stage)
                        for other in range(1, supers):
                            plane_stage(other, 0)
                        for acc in (gate_acc, up_acc, down_acc):
                            acc[...] = jnp.zeros(acc.shape, F32)
                if i == 2:
                    @pl.when(s == 0)
                    def _():
                        for stage in (1, 2):
                            for other in range(1, supers):
                                plane_stage(other, stage)

            for p in range(PLANE):
                if p % 4 == i:
                    @pl.when(s == 1 + p // 4)
                    def _():
                        mix(p)

            back, at_step = (i - lag) // 4, (i - lag) % 4

            @pl.when((s + back >= 0) & (s + back < supers))
            def _():
                compute(s + back, at_step)

    column = lax.broadcasted_iota(jnp.int32, (group, LANES), 1)

    @pl.loop(0, PLANE)
    def _(p):
        rows = pl.ds(pl.multiple_of(p * group, 16), group)
        for j in range(owned):
            mine = slice(j * group, (j + 1) * group)
            gate_pre, up_pre, upward = gate_acc[j, rows, :], up_acc[j, rows, :], down_acc[j, rows, :]
            sigma = 1.0 / (1.0 + jnp.exp(-gate_pre))
            silu_val = gate_pre * sigma
            up_delta = upward * silu_val
            pick_gate = jnp.sum(up_delta * up_pre, axis=1, keepdims=True)
            gate_delta = upward * up_pre * sigma * (1.0 + gate_pre * (1.0 - sigma))
            for d in range(deltas):
                columns = slice(d * cw, (d + 1) * cw)
                xline[d, p, mine, :] = gate_delta[:, columns].astype(BF)
                xline[deltas + d, p, mine, :] = up_delta[:, columns].astype(BF)
            high = pick_gate.astype(BF).astype(F32)
            low = pick_gate - high
            both = jnp.where(column == 0, high, jnp.where(column == 1, low, 0.0))
            gsend[p, mine, :] = both.astype(BF)

    @pl.loop(supers * 3 - ring, supers * 3)
    def _(a):
        for b in range(1, PLANE):
            line_give(a, b).wait_send()

    returns = half

    def give(c, b):
        return remote(
            packed_line.at[c, flipped(r, b)], rrecv.at[c, r], rs_sem.at[c, b], rr_sem.at[c, r],
            at(0, b),
        )

    def keep(c):
        return pltpu.make_async_copy(packed_line.at[c, r], rrecv.at[c, r], rs_sem.at[c, 0])

    def give_gate(b):
        return remote(
            gsend.at[flipped(r, b)], grecv.at[r], gs_sem.at[b], gr_sem.at[r], at(0, b)
        )

    keep_gate = pltpu.make_async_copy(gsend.at[r], grecv.at[r], gs_sem.at[0])

    def home(c, k):
        slot = flipped(z, k)
        return remote(
            zsend.at[c, slot], zrecv.at[c, z], hs_sem.at[c, k], hr_sem.at[c, z], at(k, 0)
        )

    def home_gate(k):
        slot = flipped(z, k)
        return remote(
            zgsend.at[slot], zgrecv.at[z], hgs_sem.at[k], hgr_sem.at[z], at(k, 0)
        )

    for b in range(1, PLANE):
        give_gate(b).start()
    keep_gate.start()

    @pl.loop(0, returns // 2)
    def _(pair):
        for slot in range(2):
            c = 2 * pair + slot

            @pl.when(c + 1 < returns)
            def _():
                for load in first_loads(c + 1, 1 - slot):
                    load.start()

            for load in first_loads(c, slot):
                load.wait()
            for j in range(owned):
                mine = slice(j * group, (j + 1) * group)
                total = None
                for d in range(2 * deltas):
                    weight = (gate_w if d < deltas else up_w)[slot, j]
                    columns = slice((d % deltas) * cw, (d % deltas + 1) * cw)
                    rows = xline[d, :, mine, :].reshape(PLANE * group, cw)
                    term = dot_t(rows, weight[:, columns])
                    total = term if total is None else total + term
                packed_line[c, :, mine, :] = total.astype(BF).reshape(PLANE, group, cw)
            for b in (6, 7, 2, 4, 3, 5, 1):
                give(c, b).start()
            keep(c).start()

    own = pl.ds(pl.multiple_of(z * tok, tok), tok)

    @pl.loop(0, returns)
    def _(c):
        keep(c).wait()
        for b in range(1, PLANE):
            other = flipped(r, b)
            remote(
                rrecv.at[c, other], rrecv.at[c, other], rs_sem.at[c, 0], rr_sem.at[c, other],
                at(0, 1),
            ).wait_recv()
        rows = rrecv[c].reshape(slots, cw)
        total = dot(mix_high[...], rows) + dot(mix_low[...], rows)
        zsend[c] = total.astype(BF).reshape(planes, tok, cw)
        for k in range(planes - 1, 0, -1):
            home(c, k).start()
        columns = pl.ds(pl.multiple_of(c * cw, cw), cw)
        out_ref[:, columns] = dot(mix_high[own, :], rows) + dot(mix_low[own, :], rows)

        @pl.when(c == 1)
        def _():
            keep_gate.wait()
            for b in range(1, PLANE):
                other = flipped(r, b)
                remote(
                    grecv.at[other], grecv.at[other], gs_sem.at[0], gr_sem.at[other], at(0, 1)
                ).wait_recv()
            picked = grecv[...].reshape(slots, LANES).astype(F32)
            lane_of = lax.broadcasted_iota(jnp.int32, (slots, LANES), 1)
            number = slot_numbers((slots, LANES), 0, cap, planes)[0].astype(jnp.int32)
            here = lane_of == number + z * PLANE * owned
            high = jnp.sum(jnp.where(lane_of == 0, picked, 0.0), axis=1, keepdims=True)
            low = jnp.sum(jnp.where(lane_of == 1, picked, 0.0), axis=1, keepdims=True)
            high = jnp.where(here, high, 0.0).astype(BF)
            low = jnp.where(here, low, 0.0).astype(BF)
            gates = dot(marks[...], high) + dot(marks[...], low)
            zgsend[...] = gates.reshape(planes, tok, LANES)
            for k in range(1, planes):
                home_gate(k).start()

    @pl.loop(0, returns)
    def _(c):
        columns = pl.ds(pl.multiple_of(c * cw, cw), cw)
        total = out_ref[:, columns]
        for k in range(1, planes):
            slot = flipped(z, k)
            remote(
                zrecv.at[c, slot], zrecv.at[c, slot], hs_sem.at[c, 0], hr_sem.at[c, slot],
                at(1, 0),
            ).wait_recv()
            total = total + zrecv[c, slot].astype(F32)
        out_ref[:, columns] = total

    total = zgsend[z]
    for k in range(1, planes):
        slot = flipped(z, k)
        remote(
            zgrecv.at[slot], zgrecv.at[slot], hgs_sem.at[0], hgr_sem.at[slot], at(1, 0)
        ).wait_recv()
        total = total + zgrecv[slot]
    gate_out[...] = total

    for e in range(len(edges)):
        line_hop(*ranks_of, (), e).wait_send()
    for b in range(1, PLANE):
        ranks_hop(b).wait_send()
        give_gate(b).wait_send()
    for k in range(1, planes):
        home_gate(k).wait_send()

    @pl.loop(0, 3 * supers)
    def _(a):
        for e in range(len(edges)):
            line_hop(*data, (a,), e).wait_send()

    @pl.loop(0, supers)
    def _(s):
        for stage in hops:
            for hop in stage:
                plane_hop(s, hop).wait_send()
        for k in range(1, planes):
            plane_give(s, k).wait_send()

    @pl.loop(0, returns)
    def _(c):
        for b in range(1, PLANE):
            give(c, b).wait_send()
        for k in range(1, planes):
            home(c, k).wait_send()


def fused(planes, cap, tokens, cotangent, aux, gate_weight, up_weight, down_weight):
    tok, width = tokens.shape
    owned, _, ff = gate_weight.shape
    cw = COLUMNS
    half = width // cw
    supers = 2 * half // 4
    line = 3 * supers
    ring = half
    group = planes * cap
    part, rows = owned * group, PLANE * group
    part_plane = owned * PLANE * cap
    slots = PLANE * part
    edges = len(line_edges(planes))
    vmem = pl.BlockSpec(memory_space=pltpu.VMEM)
    hbm = pl.BlockSpec(memory_space=pl.ANY)
    dma = pltpu.SemaphoreType.DMA
    return pl.pallas_call(
        functools.partial(fused_kernel, planes, cap, ring, 5),
        out_shape=(
            jax.ShapeDtypeStruct((tok, width), F32),
            jax.ShapeDtypeStruct((tok, LANES), F32),
        ),
        in_specs=[hbm, hbm, vmem, hbm, hbm, hbm],
        out_specs=(vmem, vmem),
        scratch_shapes=[
            pltpu.VMEM((line, planes, tok, cw), BF),
            pltpu.VMEM((supers, PLANE, tok, cw), BF),
            pltpu.VMEM((planes,) + aux.shape, BF),
            pltpu.VMEM((PLANE, tok, LANES), BF),
            pltpu.VMEM((PLANE * part, planes * tok), BF),
            pltpu.VMEM((planes * part_plane, PLANE * tok), BF),
            pltpu.VMEM((rows, rows), BF),
            pltpu.VMEM((ring, PLANE, part, cw), BF),
            pltpu.VMEM((supers, planes, part_plane, cw), BF),
            pltpu.VMEM((line, PLANE, part, cw), BF),
            pltpu.VMEM((supers, planes, part_plane, cw), BF),
            pltpu.VMEM((owned, rows, ff), F32),
            pltpu.VMEM((owned, rows, ff), F32),
            pltpu.VMEM((owned, rows, ff), F32),
            pltpu.VMEM((2, owned, cw, ff), BF),
            pltpu.VMEM((2, owned, cw, ff), BF),
            pltpu.VMEM((2, owned, ff, cw), BF),
            pltpu.VMEM((half, PLANE, part, cw), BF),
            pltpu.VMEM((PLANE, part, LANES), BF),
            pltpu.VMEM((PLANE, part, LANES), BF),
            pltpu.VMEM((planes * tok, slots), BF),
            pltpu.VMEM((planes * tok, slots), BF),
            pltpu.VMEM((planes * tok, slots), BF),
            pltpu.VMEM((half, planes, tok, cw), BF),
            pltpu.VMEM((half, planes, tok, cw), BF),
            pltpu.VMEM((planes, tok, LANES), F32),
            pltpu.VMEM((planes, tok, LANES), F32),
            dma((3, 2)),
            dma((4 * supers,)),
            dma((2,)),
            dma((edges,)),
            dma((planes,)),
            dma((PLANE,)),
            dma((PLANE,)),
            dma((line, edges)),
            dma((line, planes)),
            dma((supers, 7)),
            dma((supers, PLANE)),
            dma((ring, PLANE)),
            dma((line, PLANE)),
            dma((supers, planes)),
            dma((supers, planes)),
            dma((line,)),
            dma((half, PLANE)),
            dma((half, PLANE)),
            dma((PLANE,)),
            dma((PLANE,)),
            dma((half, planes)),
            dma((half, planes)),
            dma((planes,)),
            dma((planes,)),
        ],
        compiler_params=pltpu.CompilerParams(
            collective_id=0, has_side_effects=True, vmem_limit_bytes=63 * 2**20
        ),
    )(tokens, cotangent, aux, gate_weight, up_weight, down_weight)


def by_planes(planes, tokens, cotangent, routing, expert_ids, gate_weight, up_weight, down_weight):
    owned = gate_weight.shape[0]
    experts = owned * planes * PLANE
    tok, top = expert_ids.shape
    cap = 5 * tok * top // (4 * experts)
    onehot = expert_ids[:, :, None] == jnp.arange(LANES, dtype=jnp.int32)[None, None, :]
    picked = jnp.any(onehot, axis=1)
    row = jnp.arange(tok, dtype=jnp.int32)
    lower = (row[:, None] > row[None, :]).astype(BF)
    rank = jnp.where(picked, dot(lower, picked.astype(BF)), -1.0).astype(BF)
    amount = jnp.sum(jnp.where(onehot, routing[:, :, None], 0.0), axis=1)
    amount_high, amount_low = split_two(amount)
    aux = jnp.concatenate([rank, amount_high, amount_low], axis=1)
    input_grad, gate_sum = fused(
        planes, cap, tokens, cotangent, aux, gate_weight, up_weight, down_weight
    )
    gate_grad = jnp.sum(jnp.where(onehot, gate_sum[:, None, :], 0.0), axis=2)
    return input_grad, gate_grad


def local(tokens, cotangent, routing, expert_ids, gate_weight, up_weight, down_weight):
    count = lax.axis_size("ep")
    owned = gate_weight.shape[0]
    experts = owned * count
    tok_rows, top = expert_ids.shape
    width = tokens.shape[1]
    cap = 5 * tok_rows * top // (4 * experts)
    slots = experts * cap

    onehot = expert_ids[:, :, None] == jnp.arange(experts, dtype=jnp.int32)[None, None, :]
    picked = jnp.any(onehot, axis=1)
    row = jnp.arange(tok_rows, dtype=jnp.int32)
    lower = (row[:, None] > row[None, :]).astype(BF)
    before = dot(lower, picked.astype(BF))
    rank = jnp.where(picked, before, -1.0).astype(BF)
    slot = jnp.arange(slots, dtype=jnp.int32)
    spread = (slot[:, None] // cap == jnp.arange(experts, dtype=jnp.int32)[None, :]).astype(BF)
    place = (slot % cap).astype(F32)
    rank_of = lax.dot_general(spread, rank, (((1,), (1,)), ((), ())), preferred_element_type=F32)
    choose = (rank_of == place[:, None]).astype(BF)
    rank_back = lax.dot_general(rank, spread, (((1,), (1,)), ((), ())), preferred_element_type=F32)
    choose_back = rank_back == place[None, :]

    def exchange(value):
        return lax.all_to_all(value, "ep", split_axis=0, concat_axis=0, tiled=True)

    def by_expert(value):
        value = value.reshape(count, owned, cap, value.shape[1])
        return value.transpose(1, 0, 2, 3).reshape(owned, count * cap, value.shape[3])

    def by_source(value):
        value = value.reshape(owned, count, cap, value.shape[2])
        return value.transpose(1, 0, 2, 3).reshape(slots, value.shape[3])

    inputs = by_expert(exchange(dot(choose, tokens).astype(BF)))
    grads_in = by_expert(exchange(dot(choose, cotangent).astype(BF)))
    gate_pre = jnp.einsum("erd,edf->erf", inputs, gate_weight, preferred_element_type=F32)
    up_pre = jnp.einsum("erd,edf->erf", inputs, up_weight, preferred_element_type=F32)
    upward = jnp.einsum("erd,efd->erf", grads_in, down_weight, preferred_element_type=F32)
    sigma = jax.nn.sigmoid(gate_pre)
    silu_val = gate_pre * sigma
    pick_gate = jnp.sum(silu_val * up_pre * upward, axis=2, keepdims=True)
    gate_delta = (upward * up_pre * sigma * (1.0 + gate_pre * (1.0 - sigma))).astype(BF)
    up_delta = (upward * silu_val).astype(BF)
    deltas = jnp.concatenate([gate_delta, up_delta], axis=2)
    joined = jnp.concatenate([gate_weight, up_weight], axis=2)

    half = width // 2
    gate_high, gate_low = split_two(pick_gate)
    lane = jnp.arange(128, dtype=jnp.int32)[None, None, :]
    gate_cols = jnp.where(lane == 0, gate_high, jnp.where(lane == 1, gate_low, jnp.zeros((), BF)))
    first = jnp.einsum("erf,edf->erd", deltas, joined[:, :half], preferred_element_type=F32).astype(BF)
    second = jnp.einsum("erf,edf->erd", deltas, joined[:, half:], preferred_element_type=F32).astype(BF)
    back_a = exchange(by_source(jnp.concatenate([first, gate_cols], axis=2)))
    back_b = exchange(by_source(second))

    amount = jnp.sum(jnp.where(onehot, routing[:, :, None], 0.0), axis=1)
    amount_high, amount_low = split_two(amount)
    zero = jnp.zeros((), BF)

    def mix(part):
        wide = lax.dot_general(part, spread, (((1,), (1,)), ((), ())), preferred_element_type=F32)
        return jnp.where(choose_back, wide.astype(BF), zero)

    mixing = jnp.concatenate([mix(amount_high), mix(amount_low)], axis=0)

    def combine(value):
        both = dot(mixing, value)
        return both[:tok_rows] + both[tok_rows:]

    weighted = jnp.concatenate([combine(back_a[:, :half]), combine(back_b)], axis=1)
    gates = back_a[:, half:half + 2].T

    def gate_part(i):
        return dot(jnp.where(choose_back, gates[i][None, :], zero), spread)

    gate_sum = gate_part(0) + gate_part(1)
    gate_grad = jnp.sum(jnp.where(onehot, gate_sum[:, None, :], 0.0), axis=2)
    input_grad = lax.psum_scatter(weighted, "hid", scatter_dimension=1, tiled=True)
    return (input_grad, lax.psum(gate_grad, "hid"))


def solution(mesh):
    placed = (
        P(("rep", "ep"), None),
        P(("rep", "ep"), None),
        P(("rep", "ep"), None),
        P(("rep", "ep"), None),
        P("ep", None, "hid"),
        P("ep", None, "hid"),
        P("ep", "hid", None),
    )
    count = mesh.shape["ep"]
    planes = count // PLANE
    direct = (
        mesh.shape["rep"] * mesh.shape["hid"] == 1
        and count % PLANE == 0
        and planes > 1
        and planes & (planes - 1) == 0
    )

    def run(tokens, cotangent, routing, expert_ids, gate_weight, *rest):
        tok, top = expert_ids.shape
        owned, width, ff = gate_weight.shape
        cap = 5 * tok * top // (4 * owned * count)
        fits = (
            direct
            and owned * count <= LANES
            and planes * cap % 16 == 0
            and tok % 16 == 0
            and width % (4 * COLUMNS) == 0
            and ff % COLUMNS == 0
            and 2 * ff // COLUMNS <= 6 * width // (4 * COLUMNS)
        )
        body = functools.partial(by_planes, planes) if fits else local
        return body(tokens, cotangent, routing, expert_ids, gate_weight, *rest)

    return jax.shard_map(
        run,
        mesh=mesh,
        in_specs=placed,
        out_specs=(P(("rep", "ep"), "hid"), P(("rep", "ep"), None)),
        check_vma=False,
    )
```

```python
import functools

import jax
import jax.numpy as jnp
from jax import lax
from jax.experimental import pallas as pl
from jax.experimental.pallas import tpu as pltpu
from jax.sharding import PartitionSpec as P

BF = jnp.bfloat16
F32 = jnp.float32
PLANE = 8
LANES = 128
COLUMNS = 256


def dot(a, b):
    return jnp.dot(a, b, preferred_element_type=F32)


def dot_t(a, b):
    return lax.dot_general(a, b, (((1,), (1,)), ((), ())), preferred_element_type=F32)


def split_two(value):
    high = lax.reduce_precision(value, 8, 7)
    return high.astype(BF), (value - high).astype(BF)


def flipped(value, bits):
    result, weight = value * 0, 1
    while weight <= bits:
        digit = lax.rem(lax.div(value, weight), 2)
        result = result + weight * ((1 - digit) if bits & weight else digit)
        weight *= 2
    return result + weight * lax.div(value, weight)


def line_edges(planes):
    edges = []
    for k in range(planes):
        b = 1
        while b < planes and (k == 0 or b < (k & -k)):
            edges.append((k, b))
            b *= 2
    return edges


def remote(source, target, send_sem, recv_sem, other):
    return pltpu.make_async_remote_copy(
        src_ref=source,
        dst_ref=target,
        send_sem=send_sem,
        recv_sem=recv_sem,
        device_id={"ep": other},
        device_id_type=pl.DeviceIdType.MESH,
    )


def greet(partners, meanwhile=None):
    barrier = pltpu.get_barrier_semaphore()
    for other in partners:
        pl.semaphore_signal(
            barrier, inc=1, device_id={"ep": other}, device_id_type=pl.DeviceIdType.MESH
        )
    if meanwhile is not None:
        meanwhile()
    pl.semaphore_wait(barrier, len(partners))


def slot_numbers(shape, axis, cap, planes):
    number = lax.broadcasted_iota(jnp.int32, shape, axis).astype(F32)
    block = jnp.floor((number + 0.5) * (1.0 / cap))
    expert = jnp.floor((block + 0.5) * (1.0 / planes))
    return expert, block - expert * planes, number - block * cap


def fused_kernel(
    planes, cap, ring, lag,
    tokens_ref, cotangent_ref, weights_ref, ids_ref, gate_hbm, up_hbm, down_hbm,
    out_ref, gate_out,
    zbuf, pbuf, zrank, zamount, paux, choose_line, choose_plane, reorder, packed_line, packed_plane,
    xline, xplane, gate_acc, up_acc, down_acc, gate_w, up_w, down_w,
    rrecv, gsend, grecv, marks, mix_high, mix_low, zsend, zrecv, zgsend, zgrecv,
    load_sem, own_sem, zks_sem, zkr_sem, zas_sem, zar_sem, pas_sem, par_sem, zs_sem, zr_sem, ps_sem, pr_sem,
    ls_sem, lr_sem, bs_sem, br_sem, keep_sem, rs_sem, rr_sem, gs_sem, gr_sem, hs_sem, hr_sem,
    hgs_sem, hgr_sem,
):
    me = lax.axis_index("ep")
    z, r = lax.div(me, PLANE), lax.rem(me, PLANE)
    supers, _, tok, cw = pbuf.shape
    steps = 4 * supers
    half = steps // 2
    owned, ff = gate_w.shape[1], gate_w.shape[3]
    group = planes * cap
    part = owned * group
    wide = PLANE * cap
    part_plane = owned * wide
    slots = PLANE * part
    deltas = ff // cw
    edges = line_edges(planes)

    def at(k, bits):
        return flipped(z, k) * PLANE + flipped(r, bits)

    core = lax.rem(r, 2)
    along_x, along_y, across, twin = (flipped(r, b) for b in (2, 4, 6, 1))
    near = along_x + core * (along_y - along_x)
    then = along_y + core * (along_x - along_y)

    def line_index(s, i):
        return 3 * s + (0, 1, None, 2)[i]

    for q in range(steps):
        source = tokens_ref if q < half else cotangent_ref
        columns = pl.ds((q % half) * cw, cw)
        s, i = q // 4, q % 4
        target = pbuf.at[s, r] if i == 2 else zbuf.at[line_index(s, i), z]
        pltpu.make_async_copy(source.at[:, columns], target, own_sem.at[q]).start()

    def first_loads(n, slot):
        depth = pl.ds(pl.multiple_of(n * cw, cw), cw)
        return [
            pltpu.make_async_copy(w.at[:, depth, :], buf.at[slot], load_sem.at[k, slot])
            for k, (w, buf) in enumerate(((gate_hbm, gate_w), (up_hbm, up_w)))
        ]

    def down_load(n, slot):
        depth = pl.ds(pl.multiple_of((n - half) * cw, cw), cw)
        return pltpu.make_async_copy(
            down_hbm.at[:, :, depth], down_w.at[slot], load_sem.at[2, slot]
        )

    for load in first_loads(0, 0):
        load.start()

    top = ids_ref.shape[0]
    expert_row = lax.broadcasted_iota(jnp.int32, (LANES, tok), 0)
    named = jnp.zeros((LANES, tok), F32)
    amount = jnp.zeros((LANES, tok), F32)
    for k in range(top):
        hit = expert_row == ids_ref[k:k + 1, :]
        named = jnp.where(hit, 1.0, named)
        amount = jnp.where(hit, weights_ref[k:k + 1, :], amount)
    earlier = lax.broadcasted_iota(jnp.int32, (tok, tok), 0)
    earlier = earlier < lax.broadcasted_iota(jnp.int32, (tok, tok), 1)
    rank = dot(named.astype(BF), jnp.where(earlier, 1.0, 0.0).astype(BF))
    rank = jnp.where(named > 0.0, rank, -1.0).T.astype(BF)
    zrank[z] = rank
    paux[r] = rank
    amount = amount.T
    amount_high = amount.astype(BF)
    zamount[z, :, :LANES] = amount_high
    zamount[z, :, LANES:] = (amount - amount_high.astype(F32)).astype(BF)

    def prepare():
        for acc in (gate_acc, up_acc, down_acc):
            acc[...] = jnp.zeros(acc.shape, F32)
        size = PLANE * group
        _, from_z, place = slot_numbers((size, size), 0, cap, planes)
        origin = slot_numbers((size, size), 0, cap, planes)[0]
        column = lax.broadcasted_iota(jnp.int32, (size, size), 1).astype(F32)
        wanted = (from_z * PLANE + origin) * cap + place
        reorder[...] = jnp.where(column == wanted, 1.0, 0.0).astype(BF)

    greet([at(k, 0) for k in range(1, planes)] + [at(0, b) for b in range(1, PLANE)], prepare)

    def line_hop(buf, sems, rems, index, e):
        k, b = edges[e]
        slot = flipped(z, k)
        return remote(
            buf.at[index + (slot,)], buf.at[index + (slot,)], sems.at[index + (e,)],
            rems.at[index + (slot,)], at(b, 0),
        )

    def line_arrived(buf, sems, rems, index, k):
        slot = flipped(z, k)
        remote(
            buf.at[index + (slot,)], buf.at[index + (slot,)], sems.at[index + (0,)],
            rems.at[index + (slot,)], at(1, 0),
        ).wait_recv()

    forwarded = sorted({k for k, b in edges if k}, reverse=True)
    plain = [k for k in range(1, planes) if k not in forwarded]
    data = (zbuf, zs_sem, zr_sem)

    def line_start(kind, index):
        for e, (k, b) in enumerate(edges):
            if k == 0:
                line_hop(*kind, index, e).start()

    def line_forward(kind, index):
        for wanted in forwarded:
            line_arrived(*kind, index, wanted)
            for e, (k, b) in enumerate(edges):
                if k == wanted:
                    line_hop(*kind, index, e).start()

    def line_rest(kind, index):
        for k in plain:
            line_arrived(*kind, index, k)

    def straight(buf, sems, rems, k):
        return remote(buf.at[z], buf.at[z], sems.at[k], rems.at[z], at(k, 0))

    def straight_arrived(buf, sems, rems):
        for k in range(1, planes):
            slot = flipped(z, k)
            remote(
                buf.at[slot], buf.at[slot], sems.at[0], rems.at[slot], at(1, 0)
            ).wait_recv()

    def first_straight(k):
        return remote(
            zbuf.at[0, z], zbuf.at[0, z], zs_sem.at[0, k - 1], zr_sem.at[0, z], at(k, 0)
        )

    line_ranks, line_amounts = (zrank, zks_sem, zkr_sem), (zamount, zas_sem, zar_sem)

    def line_own(s, i):
        a = line_index(s, i)
        pltpu.make_async_copy(zbuf.at[a, z], zbuf.at[a, z], own_sem.at[4 * s + i]).wait()
        line_start(data, (a,))

    hops = [
        [(r, near, 0), (r, then, 1), (r, twin, 2)],
        [(near, then, 3), (near, twin, 4), (then, twin, 5)],
        [(across, twin, 6)],
    ]

    def plane_hop(s, hop):
        slot, other, e = hop
        return remote(
            pbuf.at[s, slot], pbuf.at[s, slot], ps_sem.at[s, e], pr_sem.at[s, slot],
            z * PLANE + other,
        )

    def plane_arrived(s, slot):
        remote(
            pbuf.at[s, slot], pbuf.at[s, slot], ps_sem.at[s, 0], pr_sem.at[s, slot], at(0, 1)
        ).wait_recv()

    def plane_stage(s, stage):
        if stage == 0:
            pltpu.make_async_copy(pbuf.at[s, r], pbuf.at[s, r], own_sem.at[4 * s + 2]).wait()
        elif stage == 1:
            plane_arrived(s, near)
            plane_arrived(s, then)
        elif stage == 2:
            plane_arrived(s, across)
        else:
            for b in (1, 3, 5, 7):
                plane_arrived(s, flipped(r, b))
            return
        for hop in hops[stage]:
            plane_hop(s, hop).start()

    def ranks_hop(b):
        return remote(
            paux.at[r], paux.at[r], pas_sem.at[b], par_sem.at[r], at(0, b)
        )

    for k in range(1, planes):
        straight(*line_ranks, k).start()
    pltpu.make_async_copy(zbuf.at[0, z], zbuf.at[0, z], own_sem.at[0]).wait()
    for k in range(1, planes):
        first_straight(k).start()
    for b in range(1, PLANE):
        ranks_hop(b).start()
    plane_stage(0, 0)
    line_own(0, 1)
    for s in range(1, supers):
        plane_stage(s, 0)

    token = lax.broadcasted_iota(jnp.int32, (part, planes * tok), 1).astype(F32)
    token_z = jnp.floor((token + 0.5) * (1.0 / tok))
    _, slot_z, place = slot_numbers((part, planes * tok), 0, cap, planes)
    same_z = token_z == slot_z
    lane = lax.broadcasted_iota(jnp.int32, (part, LANES), 1)
    expert = slot_numbers((part, LANES), 0, cap, planes)[0].astype(jnp.int32)
    straight_arrived(*line_ranks)
    ranks = zrank[...].reshape(planes * tok, LANES)

    @pl.loop(0, PLANE)
    def _(p):
        first = (z * PLANE + p) * owned
        spread = jnp.where(lane == expert + first, 1.0, 0.0).astype(BF)
        rank_of = dot_t(spread, ranks)
        rows = pl.ds(pl.multiple_of(p * part, 16), part)
        choose_line[rows, :] = jnp.where(same_z & (rank_of == place), 1.0, 0.0).astype(BF)

    def choose_in_plane():
        for b in range(1, PLANE):
            other = flipped(r, b)
            remote(
                paux.at[other], paux.at[other], pas_sem.at[0], par_sem.at[other], at(0, 1)
            ).wait_recv()
        token = lax.broadcasted_iota(jnp.int32, (part_plane, PLANE * tok), 1).astype(F32)
        token_from = jnp.floor((token + 0.5) * (1.0 / tok))
        _, slot_from, place = slot_numbers((part_plane, PLANE * tok), 0, cap, PLANE)
        same = token_from == slot_from
        lane = lax.broadcasted_iota(jnp.int32, (part_plane, LANES), 1)
        expert = slot_numbers((part_plane, LANES), 0, cap, PLANE)[0].astype(jnp.int32)
        ranks = paux[...].reshape(PLANE * tok, LANES)

        @pl.loop(0, planes)
        def _(k):
            first = (k * PLANE + r) * owned
            spread = jnp.where(lane == expert + first, 1.0, 0.0).astype(BF)
            rank_of = dot_t(spread, ranks)
            rows = pl.ds(pl.multiple_of(k * part_plane, 16), part_plane)
            choose_plane[rows, :] = jnp.where(same & (rank_of == place), 1.0, 0.0).astype(BF)


    def line_give(a, b):
        other = flipped(r, b)
        slot = lax.rem(a, ring)
        return remote(
            packed_line.at[slot, other], xline.at[a, r], ls_sem.at[slot, other], lr_sem.at[a, r],
            at(0, b),
        )

    def line_keep(a):
        return pltpu.make_async_copy(
            packed_line.at[lax.rem(a, ring), r], xline.at[a, r], keep_sem.at[a]
        )

    def pack_line(a):
        line_rest(data, (a,))

        @pl.when(a == 0)
        def _():
            for k in forwarded:
                line_arrived(*data, (0,), k)

        @pl.when(a >= ring)
        def _():
            for b in range(1, PLANE):
                line_give(a - ring, b).wait_send()

        picked = dot(choose_line[...], zbuf[a].reshape(planes * tok, cw)).astype(BF)
        packed_line[lax.rem(a, ring)] = picked.reshape(PLANE, part, cw)
        for b in (6, 7, 2, 4, 3, 5, 1):
            line_give(a, b).start()
        line_keep(a).start()

    def plane_give(s, k):
        other = flipped(z, k)
        return remote(
            packed_plane.at[s, other], xplane.at[s, z], bs_sem.at[s, k], br_sem.at[s, z], at(k, 0)
        )

    def plane_keep(s):
        return pltpu.make_async_copy(packed_plane.at[s, z], xplane.at[s, z], bs_sem.at[s, 0])

    def pack_plane(s):
        picked = dot(choose_plane[...], pbuf[s].reshape(PLANE * tok, cw)).astype(BF)
        packed_plane[s] = picked.reshape(planes, part_plane, cw)
        for k in range(planes - 1, 0, -1):
            plane_give(s, k).start()
        plane_keep(s).start()

    def rows_line(a):
        line_keep(a).wait()
        for b in range(1, PLANE):
            other = flipped(r, b)
            remote(
                xline.at[a, other], xline.at[a, other], ls_sem.at[0, 0], lr_sem.at[a, other],
                at(0, 1),
            ).wait_recv()
        return [
            xline[a, :, j * group:(j + 1) * group, :].reshape(PLANE * group, cw)
            for j in range(owned)
        ]

    def rows_plane(s):
        plane_keep(s).wait()
        for k in range(1, planes):
            other = flipped(z, k)
            remote(
                xplane.at[s, other], xplane.at[s, other], bs_sem.at[s, 0], br_sem.at[s, other],
                at(1, 0),
            ).wait_recv()
        return [
            dot(
                reorder[...],
                xplane[s, :, j * wide:(j + 1) * wide, :].reshape(PLANE * group, cw),
            ).astype(BF)
            for j in range(owned)
        ]

    def compute(s, i):
        n = 4 * s + i
        slot = i % 2
        rows = rows_plane(s) if i == 2 else rows_line(line_index(s, i))

        @pl.when(n + 1 < half)
        def _():
            for load in first_loads(n + 1, 1 - slot):
                load.start()

        @pl.when((n + 1 >= half) & (n + 1 < steps))
        def _():
            down_load(n + 1, 1 - slot).start()

        @pl.when(n + 1 == steps)
        def _():
            for load in first_loads(0, 1 - slot):
                load.start()

        @pl.when(n < half)
        def _():
            for load in first_loads(n, slot):
                load.wait()
            for j in range(owned):
                gate_acc[j] += dot(rows[j], gate_w[slot, j])
                up_acc[j] += dot(rows[j], up_w[slot, j])

        @pl.when(n >= half)
        def _():
            down_load(n, slot).wait()
            for j in range(owned):
                down_acc[j] += dot_t(rows[j], down_w[slot, j])

    def mix(p):
        _, slot_z, place = slot_numbers((tok, part), 1, cap, planes)
        first = (z * PLANE + p) * owned
        spread = jnp.where(lane == expert + first, 1.0, 0.0).astype(BF)
        columns = slice(p * part, (p + 1) * part)
        for k in range(planes):
            rows = slice(k * tok, (k + 1) * tok)
            values = zamount[k]
            rank_of = dot_t(zrank[k], spread)
            hit = (rank_of == place) & (slot_z == float(k))
            marks[rows, columns] = jnp.where(hit, 1.0, 0.0).astype(BF)
            high = dot_t(values[:, :LANES], spread)
            low = dot_t(values[:, LANES:], spread)
            mix_high[rows, columns] = jnp.where(hit, high, 0.0).astype(BF)
            mix_low[rows, columns] = jnp.where(hit, low, 0.0).astype(BF)

    @pl.loop(0, supers + 2)
    def _(s):
        for i in range(4):
            @pl.when(s < supers)
            def _():
                if i == 2:
                    @pl.when(s == 0)
                    def _():
                        choose_in_plane()

                    plane_stage(s, 3)
                    pack_plane(s)
                else:
                    early = {0: ((0, 3), (1, 0)), 1: ((1, 1), (1, 3)), 3: ((2, 0), (2, 1))}[i]
                    later = {0: (s + 1, 3), 1: (s + 2, 0), 3: (s + 2, 1)}[i]
                    follow = {0: (s, 3), 1: (s + 1, 0), 3: (s + 1, 1)}[i]

                    @pl.when(s == 0)
                    def _():
                        for item in early:
                            if item[0] < supers:
                                line_own(*item)

                    @pl.when((s >= 1) & (later[0] < supers))
                    def _():
                        line_own(*later)

                    pack_line(line_index(s, i))

                    if i == 0:
                        @pl.when(s == 0)
                        def _():
                            for k in range(1, planes):
                                straight(*line_amounts, k).start()
                            line_forward(data, (1,))

                    @pl.when(follow[0] < supers)
                    def _():
                        line_forward(data, (line_index(*follow),))
                if i == 0:
                    @pl.when(s == 0)
                    def _():
                        for stage in (1, 2):
                            plane_stage(0, stage)
                if i == 2:
                    @pl.when(s == 0)
                    def _():
                        for stage in (1, 2):
                            for other in range(1, supers):
                                plane_stage(other, stage)

            for p in range(PLANE):
                if p % 4 == i:
                    @pl.when(s == 1 + p // 4)
                    def _():
                        if p == 0:
                            straight_arrived(*line_amounts)
                        mix(p)

            back, at_step = (i - lag) // 4, (i - lag) % 4

            @pl.when((s + back >= 0) & (s + back < supers))
            def _():
                compute(s + back, at_step)

    column = lax.broadcasted_iota(jnp.int32, (group, LANES), 1)

    @pl.loop(0, PLANE)
    def _(p):
        rows = pl.ds(pl.multiple_of(p * group, 16), group)
        for j in range(owned):
            mine = slice(j * group, (j + 1) * group)
            gate_pre, up_pre, upward = gate_acc[j, rows, :], up_acc[j, rows, :], down_acc[j, rows, :]
            sigma = 1.0 / (1.0 + jnp.exp(-gate_pre))
            silu_val = gate_pre * sigma
            up_delta = upward * silu_val
            pick_gate = jnp.sum(up_delta * up_pre, axis=1, keepdims=True)
            gate_delta = upward * up_pre * sigma * (1.0 + gate_pre * (1.0 - sigma))
            for d in range(deltas):
                columns = slice(d * cw, (d + 1) * cw)
                xline[d, p, mine, :] = gate_delta[:, columns].astype(BF)
                xline[deltas + d, p, mine, :] = up_delta[:, columns].astype(BF)
            high = pick_gate.astype(BF).astype(F32)
            low = pick_gate - high
            both = jnp.where(column == 0, high, jnp.where(column == 1, low, 0.0))
            gsend[p, mine, :] = both.astype(BF)

    @pl.loop(supers * 3 - ring, supers * 3)
    def _(a):
        for b in range(1, PLANE):
            line_give(a, b).wait_send()

    returns = half

    def give(c, b):
        return remote(
            packed_line.at[c, flipped(r, b)], rrecv.at[c, r], rs_sem.at[c, b], rr_sem.at[c, r],
            at(0, b),
        )

    def keep(c):
        return pltpu.make_async_copy(packed_line.at[c, r], rrecv.at[c, r], rs_sem.at[c, 0])

    def give_gate(b):
        return remote(
            gsend.at[flipped(r, b)], grecv.at[r], gs_sem.at[b], gr_sem.at[r], at(0, b)
        )

    keep_gate = pltpu.make_async_copy(gsend.at[r], grecv.at[r], gs_sem.at[0])

    def home(c, k):
        slot = flipped(z, k)
        return remote(
            zsend.at[c, slot], zrecv.at[c, z], hs_sem.at[c, k], hr_sem.at[c, z], at(k, 0)
        )

    def home_gate(k):
        slot = flipped(z, k)
        return remote(
            zgsend.at[slot], zgrecv.at[z], hgs_sem.at[k], hgr_sem.at[z], at(k, 0)
        )

    for b in range(1, PLANE):
        give_gate(b).start()
    keep_gate.start()

    @pl.loop(0, returns // 2)
    def _(pair):
        for slot in range(2):
            c = 2 * pair + slot

            @pl.when(c + 1 < returns)
            def _():
                for load in first_loads(c + 1, 1 - slot):
                    load.start()

            for load in first_loads(c, slot):
                load.wait()
            for j in range(owned):
                mine = slice(j * group, (j + 1) * group)
                total = None
                for d in range(2 * deltas):
                    weight = (gate_w if d < deltas else up_w)[slot, j]
                    columns = slice((d % deltas) * cw, (d % deltas + 1) * cw)
                    rows = xline[d, :, mine, :].reshape(PLANE * group, cw)
                    term = dot_t(rows, weight[:, columns])
                    total = term if total is None else total + term
                packed_line[c, :, mine, :] = total.astype(BF).reshape(PLANE, group, cw)
            for b in (6, 7, 2, 4, 3, 5, 1):
                give(c, b).start()
            keep(c).start()

    own = pl.ds(pl.multiple_of(z * tok, tok), tok)

    @pl.loop(0, returns)
    def _(c):
        keep(c).wait()
        for b in range(1, PLANE):
            other = flipped(r, b)
            remote(
                rrecv.at[c, other], rrecv.at[c, other], rs_sem.at[c, 0], rr_sem.at[c, other],
                at(0, 1),
            ).wait_recv()
        rows = rrecv[c].reshape(slots, cw)
        total = dot(mix_high[...], rows) + dot(mix_low[...], rows)
        zsend[c] = total.astype(BF).reshape(planes, tok, cw)
        for k in range(planes - 1, 0, -1):
            home(c, k).start()
        columns = pl.ds(pl.multiple_of(c * cw, cw), cw)
        out_ref[:, columns] = dot(mix_high[own, :], rows) + dot(mix_low[own, :], rows)

        @pl.when(c == 1)
        def _():
            keep_gate.wait()
            for b in range(1, PLANE):
                other = flipped(r, b)
                remote(
                    grecv.at[other], grecv.at[other], gs_sem.at[0], gr_sem.at[other], at(0, 1)
                ).wait_recv()
            picked = grecv[...].reshape(slots, LANES).astype(F32)
            lane_of = lax.broadcasted_iota(jnp.int32, (slots, LANES), 1)
            number = slot_numbers((slots, LANES), 0, cap, planes)[0].astype(jnp.int32)
            here = lane_of == number + z * PLANE * owned
            high = jnp.sum(jnp.where(lane_of == 0, picked, 0.0), axis=1, keepdims=True)
            low = jnp.sum(jnp.where(lane_of == 1, picked, 0.0), axis=1, keepdims=True)
            high = jnp.where(here, high, 0.0).astype(BF)
            low = jnp.where(here, low, 0.0).astype(BF)
            gates = dot(marks[...], high) + dot(marks[...], low)
            zgsend[...] = gates.reshape(planes, tok, LANES)
            for k in range(1, planes):
                home_gate(k).start()

    @pl.loop(0, returns)
    def _(c):
        columns = pl.ds(pl.multiple_of(c * cw, cw), cw)
        total = out_ref[:, columns]
        for k in range(1, planes):
            slot = flipped(z, k)
            remote(
                zrecv.at[c, slot], zrecv.at[c, slot], hs_sem.at[c, 0], hr_sem.at[c, slot],
                at(1, 0),
            ).wait_recv()
            total = total + zrecv[c, slot].astype(F32)
        out_ref[:, columns] = total

    total = zgsend[z]
    for k in range(1, planes):
        slot = flipped(z, k)
        remote(
            zgrecv.at[slot], zgrecv.at[slot], hgs_sem.at[0], hgr_sem.at[slot], at(1, 0)
        ).wait_recv()
        total = total + zgrecv[slot]
    total = total.T
    for k in range(top):
        hit = expert_row == ids_ref[k:k + 1, :]
        gate_out[k:k + 1, :] = jnp.sum(jnp.where(hit, total, 0.0), axis=0, keepdims=True)

    for k in range(1, planes):
        straight(*line_ranks, k).wait_send()
        straight(*line_amounts, k).wait_send()
        first_straight(k).wait_send()
    for b in range(1, PLANE):
        ranks_hop(b).wait_send()
        give_gate(b).wait_send()
    for k in range(1, planes):
        home_gate(k).wait_send()

    @pl.loop(1, 3 * supers)
    def _(a):
        for e in range(len(edges)):
            line_hop(*data, (a,), e).wait_send()

    @pl.loop(0, supers)
    def _(s):
        for stage in hops:
            for hop in stage:
                plane_hop(s, hop).wait_send()
        for k in range(1, planes):
            plane_give(s, k).wait_send()

    @pl.loop(0, returns)
    def _(c):
        for b in range(1, PLANE):
            give(c, b).wait_send()
        for k in range(1, planes):
            home(c, k).wait_send()


def fused(planes, cap, tokens, cotangent, weights, ids, gate_weight, up_weight, down_weight):
    tok, width = tokens.shape
    owned, _, ff = gate_weight.shape
    cw = COLUMNS
    half = width // cw
    supers = 2 * half // 4
    line = 3 * supers
    ring = half
    group = planes * cap
    part, rows = owned * group, PLANE * group
    part_plane = owned * PLANE * cap
    slots = PLANE * part
    edges = len(line_edges(planes))
    vmem = pl.BlockSpec(memory_space=pltpu.VMEM)
    hbm = pl.BlockSpec(memory_space=pl.ANY)
    dma = pltpu.SemaphoreType.DMA
    return pl.pallas_call(
        functools.partial(fused_kernel, planes, cap, ring, 5),
        out_shape=(
            jax.ShapeDtypeStruct((tok, width), F32),
            jax.ShapeDtypeStruct(ids.shape, F32),
        ),
        in_specs=[hbm, hbm, vmem, vmem, hbm, hbm, hbm],
        out_specs=(vmem, vmem),
        scratch_shapes=[
            pltpu.VMEM((line, planes, tok, cw), BF),
            pltpu.VMEM((supers, PLANE, tok, cw), BF),
            pltpu.VMEM((planes, tok, LANES), BF),
            pltpu.VMEM((planes, tok, 2 * LANES), BF),
            pltpu.VMEM((PLANE, tok, LANES), BF),
            pltpu.VMEM((PLANE * part, planes * tok), BF),
            pltpu.VMEM((planes * part_plane, PLANE * tok), BF),
            pltpu.VMEM((rows, rows), BF),
            pltpu.VMEM((ring, PLANE, part, cw), BF),
            pltpu.VMEM((supers, planes, part_plane, cw), BF),
            pltpu.VMEM((line, PLANE, part, cw), BF),
            pltpu.VMEM((supers, planes, part_plane, cw), BF),
            pltpu.VMEM((owned, rows, ff), F32),
            pltpu.VMEM((owned, rows, ff), F32),
            pltpu.VMEM((owned, rows, ff), F32),
            pltpu.VMEM((2, owned, cw, ff), BF),
            pltpu.VMEM((2, owned, cw, ff), BF),
            pltpu.VMEM((2, owned, ff, cw), BF),
            pltpu.VMEM((half, PLANE, part, cw), BF),
            pltpu.VMEM((PLANE, part, LANES), BF),
            pltpu.VMEM((PLANE, part, LANES), BF),
            pltpu.VMEM((planes * tok, slots), BF),
            pltpu.VMEM((planes * tok, slots), BF),
            pltpu.VMEM((planes * tok, slots), BF),
            pltpu.VMEM((half, planes, tok, cw), BF),
            pltpu.VMEM((half, planes, tok, cw), BF),
            pltpu.VMEM((planes, tok, LANES), F32),
            pltpu.VMEM((planes, tok, LANES), F32),
            dma((3, 2)),
            dma((4 * supers,)),
            dma((planes,)),
            dma((planes,)),
            dma((planes,)),
            dma((planes,)),
            dma((PLANE,)),
            dma((PLANE,)),
            dma((line, edges)),
            dma((line, planes)),
            dma((supers, 7)),
            dma((supers, PLANE)),
            dma((ring, PLANE)),
            dma((line, PLANE)),
            dma((supers, planes)),
            dma((supers, planes)),
            dma((line,)),
            dma((half, PLANE)),
            dma((half, PLANE)),
            dma((PLANE,)),
            dma((PLANE,)),
            dma((half, planes)),
            dma((half, planes)),
            dma((planes,)),
            dma((planes,)),
        ],
        compiler_params=pltpu.CompilerParams(
            collective_id=0, has_side_effects=True, vmem_limit_bytes=63 * 2**20
        ),
    )(tokens, cotangent, weights, ids, gate_weight, up_weight, down_weight)


def by_planes(planes, tokens, cotangent, routing, expert_ids, gate_weight, up_weight, down_weight):
    owned = gate_weight.shape[0]
    experts = owned * planes * PLANE
    tok, top = expert_ids.shape
    cap = 5 * tok * top // (4 * experts)
    input_grad, gate_grad = fused(
        planes, cap, tokens, cotangent, routing.T, expert_ids.T, gate_weight, up_weight,
        down_weight,
    )
    return input_grad, gate_grad.T


def local(tokens, cotangent, routing, expert_ids, gate_weight, up_weight, down_weight):
    count = lax.axis_size("ep")
    owned = gate_weight.shape[0]
    experts = owned * count
    tok_rows, top = expert_ids.shape
    width = tokens.shape[1]
    cap = 5 * tok_rows * top // (4 * experts)
    slots = experts * cap

    onehot = expert_ids[:, :, None] == jnp.arange(experts, dtype=jnp.int32)[None, None, :]
    picked = jnp.any(onehot, axis=1)
    row = jnp.arange(tok_rows, dtype=jnp.int32)
    lower = (row[:, None] > row[None, :]).astype(BF)
    before = dot(lower, picked.astype(BF))
    rank = jnp.where(picked, before, -1.0).astype(BF)
    slot = jnp.arange(slots, dtype=jnp.int32)
    spread = (slot[:, None] // cap == jnp.arange(experts, dtype=jnp.int32)[None, :]).astype(BF)
    place = (slot % cap).astype(F32)
    rank_of = lax.dot_general(spread, rank, (((1,), (1,)), ((), ())), preferred_element_type=F32)
    choose = (rank_of == place[:, None]).astype(BF)
    rank_back = lax.dot_general(rank, spread, (((1,), (1,)), ((), ())), preferred_element_type=F32)
    choose_back = rank_back == place[None, :]

    def exchange(value):
        return lax.all_to_all(value, "ep", split_axis=0, concat_axis=0, tiled=True)

    def by_expert(value):
        value = value.reshape(count, owned, cap, value.shape[1])
        return value.transpose(1, 0, 2, 3).reshape(owned, count * cap, value.shape[3])

    def by_source(value):
        value = value.reshape(owned, count, cap, value.shape[2])
        return value.transpose(1, 0, 2, 3).reshape(slots, value.shape[3])

    inputs = by_expert(exchange(dot(choose, tokens).astype(BF)))
    grads_in = by_expert(exchange(dot(choose, cotangent).astype(BF)))
    gate_pre = jnp.einsum("erd,edf->erf", inputs, gate_weight, preferred_element_type=F32)
    up_pre = jnp.einsum("erd,edf->erf", inputs, up_weight, preferred_element_type=F32)
    upward = jnp.einsum("erd,efd->erf", grads_in, down_weight, preferred_element_type=F32)
    sigma = jax.nn.sigmoid(gate_pre)
    silu_val = gate_pre * sigma
    pick_gate = jnp.sum(silu_val * up_pre * upward, axis=2, keepdims=True)
    gate_delta = (upward * up_pre * sigma * (1.0 + gate_pre * (1.0 - sigma))).astype(BF)
    up_delta = (upward * silu_val).astype(BF)
    deltas = jnp.concatenate([gate_delta, up_delta], axis=2)
    joined = jnp.concatenate([gate_weight, up_weight], axis=2)

    half = width // 2
    gate_high, gate_low = split_two(pick_gate)
    lane = jnp.arange(128, dtype=jnp.int32)[None, None, :]
    gate_cols = jnp.where(lane == 0, gate_high, jnp.where(lane == 1, gate_low, jnp.zeros((), BF)))
    first = jnp.einsum("erf,edf->erd", deltas, joined[:, :half], preferred_element_type=F32).astype(BF)
    second = jnp.einsum("erf,edf->erd", deltas, joined[:, half:], preferred_element_type=F32).astype(BF)
    back_a = exchange(by_source(jnp.concatenate([first, gate_cols], axis=2)))
    back_b = exchange(by_source(second))

    amount = jnp.sum(jnp.where(onehot, routing[:, :, None], 0.0), axis=1)
    amount_high, amount_low = split_two(amount)
    zero = jnp.zeros((), BF)

    def mix(part):
        wide = lax.dot_general(part, spread, (((1,), (1,)), ((), ())), preferred_element_type=F32)
        return jnp.where(choose_back, wide.astype(BF), zero)

    mixing = jnp.concatenate([mix(amount_high), mix(amount_low)], axis=0)

    def combine(value):
        both = dot(mixing, value)
        return both[:tok_rows] + both[tok_rows:]

    weighted = jnp.concatenate([combine(back_a[:, :half]), combine(back_b)], axis=1)
    gates = back_a[:, half:half + 2].T

    def gate_part(i):
        return dot(jnp.where(choose_back, gates[i][None, :], zero), spread)

    gate_sum = gate_part(0) + gate_part(1)
    gate_grad = jnp.sum(jnp.where(onehot, gate_sum[:, None, :], 0.0), axis=2)
    input_grad = lax.psum_scatter(weighted, "hid", scatter_dimension=1, tiled=True)
    return (input_grad, lax.psum(gate_grad, "hid"))


def solution(mesh):
    placed = (
        P(("rep", "ep"), None),
        P(("rep", "ep"), None),
        P(("rep", "ep"), None),
        P(("rep", "ep"), None),
        P("ep", None, "hid"),
        P("ep", None, "hid"),
        P("ep", "hid", None),
    )
    count = mesh.shape["ep"]
    planes = count // PLANE
    direct = (
        mesh.shape["rep"] * mesh.shape["hid"] == 1
        and count % PLANE == 0
        and planes > 1
        and planes & (planes - 1) == 0
    )

    def run(tokens, cotangent, routing, expert_ids, gate_weight, *rest):
        tok, top = expert_ids.shape
        owned, width, ff = gate_weight.shape
        cap = 5 * tok * top // (4 * owned * count)
        fits = (
            direct
            and owned * count <= LANES
            and planes * cap % 16 == 0
            and tok % LANES == 0
            and width % (4 * COLUMNS) == 0
            and ff % COLUMNS == 0
            and 2 * ff // COLUMNS <= 6 * width // (4 * COLUMNS)
        )
        body = functools.partial(by_planes, planes) if fits else local
        return body(tokens, cotangent, routing, expert_ids, gate_weight, *rest)

    return jax.shard_map(
        run,
        mesh=mesh,
        in_specs=placed,
        out_specs=(P(("rep", "ep"), "hid"), P(("rep", "ep"), None)),
        check_vma=False,
    )
```

```python
import functools

import jax
import jax.numpy as jnp
from jax import lax
from jax.experimental import pallas as pl
from jax.experimental.pallas import tpu as pltpu
from jax.sharding import PartitionSpec as P

BF = jnp.bfloat16
F32 = jnp.float32
PLANE = 8
LANES = 128
COLUMNS = 256
BEHIND, LAST = 2, 2


def dot(a, b):
    return jnp.dot(a, b, preferred_element_type=F32)


def dot_t(a, b):
    return lax.dot_general(a, b, (((1,), (1,)), ((), ())), preferred_element_type=F32)


def split_two(value):
    high = lax.reduce_precision(value, 8, 7)
    return high.astype(BF), (value - high).astype(BF)


def flipped(value, bits):
    result, weight = value * 0, 1
    while weight <= bits:
        digit = lax.rem(lax.div(value, weight), 2)
        result = result + weight * ((1 - digit) if bits & weight else digit)
        weight *= 2
    return result + weight * lax.div(value, weight)


def line_edges(planes):
    edges = []
    for k in range(planes):
        b = 1
        while b < planes and (k == 0 or b < (k & -k)):
            edges.append((k, b))
            b *= 2
    return edges


def remote(source, target, send_sem, recv_sem, other):
    return pltpu.make_async_remote_copy(
        src_ref=source,
        dst_ref=target,
        send_sem=send_sem,
        recv_sem=recv_sem,
        device_id={"ep": other},
        device_id_type=pl.DeviceIdType.MESH,
    )


def greet(partners, meanwhile=None):
    barrier = pltpu.get_barrier_semaphore()
    for other in partners:
        pl.semaphore_signal(
            barrier, inc=1, device_id={"ep": other}, device_id_type=pl.DeviceIdType.MESH
        )
    if meanwhile is not None:
        meanwhile()
    pl.semaphore_wait(barrier, len(partners))


def slot_numbers(shape, axis, cap, planes):
    number = lax.broadcasted_iota(jnp.int32, shape, axis).astype(F32)
    block = jnp.floor((number + 0.5) * (1.0 / cap))
    expert = jnp.floor((block + 0.5) * (1.0 / planes))
    return expert, block - expert * planes, number - block * cap


def fused_kernel(
    planes, cap, ring, lag,
    tokens_ref, cotangent_ref, weights_ref, ids_ref, gate_hbm, up_hbm, down_hbm,
    out_ref, gate_out,
    zbuf, pbuf, zrank, zamount, paux, choose_line, choose_plane, reorder, packed_line, packed_plane,
    xline, xplane, gate_acc, up_acc, down_acc, slope, gate_w, up_w, down_w,
    rrecv, gsend, grecv, marks, mix_high, mix_low, zrecv, zgsend, zgrecv,
    load_sem, own_sem, zks_sem, zkr_sem, zas_sem, zar_sem, pas_sem, par_sem, zs_sem, zr_sem, ps_sem, pr_sem,
    ls_sem, lr_sem, bs_sem, br_sem, keep_sem, rs_sem, rr_sem, gs_sem, gr_sem, hs_sem, hr_sem,
    hgs_sem, hgr_sem,
):
    me = lax.axis_index("ep")
    z, r = lax.div(me, PLANE), lax.rem(me, PLANE)
    supers, _, tok, cw = pbuf.shape
    steps = 4 * supers
    half = steps // 2
    owned, ff = gate_w.shape[1], gate_w.shape[3]
    group = planes * cap
    part = owned * group
    wide = PLANE * cap
    part_plane = owned * wide
    slots = PLANE * part
    deltas = ff // cw
    edges = line_edges(planes)

    def at(k, bits):
        return flipped(z, k) * PLANE + flipped(r, bits)

    core = lax.rem(r, 2)
    along_x, along_y, across, twin = (flipped(r, b) for b in (2, 4, 6, 1))
    near = along_x + core * (along_y - along_x)
    then = along_y + core * (along_x - along_y)

    def line_index(s, i):
        return 3 * s + (0, 1, None, 2)[i]

    for q in range(steps):
        source = tokens_ref if q < half else cotangent_ref
        columns = pl.ds((q % half) * cw, cw)
        s, i = q // 4, q % 4
        target = pbuf.at[s, r] if i == 2 else zbuf.at[line_index(s, i), z]
        pltpu.make_async_copy(source.at[:, columns], target, own_sem.at[q]).start()

    def first_loads(n, slot):
        depth = pl.ds(pl.multiple_of(n * cw, cw), cw)
        return [
            pltpu.make_async_copy(w.at[:, depth, :], buf.at[slot], load_sem.at[k, slot])
            for k, (w, buf) in enumerate(((gate_hbm, gate_w), (up_hbm, up_w)))
        ]

    def down_load(n, slot):
        depth = pl.ds(pl.multiple_of((n - half) * cw, cw), cw)
        return pltpu.make_async_copy(
            down_hbm.at[:, :, depth], down_w.at[slot], load_sem.at[2, slot]
        )

    for load in first_loads(0, 0):
        load.start()

    top = ids_ref.shape[0]
    expert_row = lax.broadcasted_iota(jnp.int32, (LANES, tok), 0)
    named = jnp.zeros((LANES, tok), F32)
    amount = jnp.zeros((LANES, tok), F32)
    for k in range(top):
        hit = expert_row == ids_ref[k:k + 1, :]
        named = jnp.where(hit, 1.0, named)
        amount = jnp.where(hit, weights_ref[k:k + 1, :], amount)
    earlier = lax.broadcasted_iota(jnp.int32, (tok, tok), 0)
    earlier = earlier < lax.broadcasted_iota(jnp.int32, (tok, tok), 1)
    rank = dot(named.astype(BF), jnp.where(earlier, 1.0, 0.0).astype(BF))
    rank = jnp.where(named > 0.0, rank, -1.0).T.astype(BF)
    zrank[z] = rank
    paux[r] = rank
    amount = amount.T
    amount_high = amount.astype(BF)
    zamount[z, :, :LANES] = amount_high
    zamount[z, :, LANES:] = (amount - amount_high.astype(F32)).astype(BF)

    def prepare():
        for acc in (gate_acc, up_acc, down_acc):
            acc[...] = jnp.zeros(acc.shape, F32)
        size = PLANE * group
        _, from_z, place = slot_numbers((size, size), 0, cap, planes)
        origin = slot_numbers((size, size), 0, cap, planes)[0]
        column = lax.broadcasted_iota(jnp.int32, (size, size), 1).astype(F32)
        wanted = (from_z * PLANE + origin) * cap + place
        reorder[...] = jnp.where(column == wanted, 1.0, 0.0).astype(BF)

    greet([at(k, 0) for k in range(1, planes)] + [at(0, b) for b in range(1, PLANE)], prepare)

    def line_hop(buf, sems, rems, index, e):
        k, b = edges[e]
        slot = flipped(z, k)
        return remote(
            buf.at[index + (slot,)], buf.at[index + (slot,)], sems.at[index + (e,)],
            rems.at[index + (slot,)], at(b, 0),
        )

    def line_arrived(buf, sems, rems, index, k):
        slot = flipped(z, k)
        remote(
            buf.at[index + (slot,)], buf.at[index + (slot,)], sems.at[index + (0,)],
            rems.at[index + (slot,)], at(1, 0),
        ).wait_recv()

    forwarded = sorted({k for k, b in edges if k}, reverse=True)
    plain = [k for k in range(1, planes) if k not in forwarded]
    data = (zbuf, zs_sem, zr_sem)

    def line_start(kind, index):
        for e, (k, b) in enumerate(edges):
            if k == 0:
                line_hop(*kind, index, e).start()

    def line_forward(kind, index):
        for wanted in forwarded:
            line_arrived(*kind, index, wanted)
            for e, (k, b) in enumerate(edges):
                if k == wanted:
                    line_hop(*kind, index, e).start()

    def line_rest(kind, index):
        for k in plain:
            line_arrived(*kind, index, k)

    def straight(buf, sems, rems, k):
        return remote(buf.at[z], buf.at[z], sems.at[k], rems.at[z], at(k, 0))

    def straight_arrived(buf, sems, rems):
        for k in range(1, planes):
            slot = flipped(z, k)
            remote(
                buf.at[slot], buf.at[slot], sems.at[0], rems.at[slot], at(1, 0)
            ).wait_recv()

    def first_straight(k):
        return remote(
            zbuf.at[0, z], zbuf.at[0, z], zs_sem.at[0, k - 1], zr_sem.at[0, z], at(k, 0)
        )

    line_ranks, line_amounts = (zrank, zks_sem, zkr_sem), (zamount, zas_sem, zar_sem)

    def line_own(s, i):
        a = line_index(s, i)
        pltpu.make_async_copy(zbuf.at[a, z], zbuf.at[a, z], own_sem.at[4 * s + i]).wait()
        line_start(data, (a,))

    hops = [
        [(r, near, 0), (r, then, 1), (r, twin, 2)],
        [(near, then, 3), (near, twin, 4), (then, twin, 5)],
        [(across, twin, 6)],
    ]

    def plane_hop(s, hop):
        slot, other, e = hop
        return remote(
            pbuf.at[s, slot], pbuf.at[s, slot], ps_sem.at[s, e], pr_sem.at[s, slot],
            z * PLANE + other,
        )

    def plane_arrived(s, slot):
        remote(
            pbuf.at[s, slot], pbuf.at[s, slot], ps_sem.at[s, 0], pr_sem.at[s, slot], at(0, 1)
        ).wait_recv()

    def plane_stage(s, stage):
        if stage == 0:
            pltpu.make_async_copy(pbuf.at[s, r], pbuf.at[s, r], own_sem.at[4 * s + 2]).wait()
        elif stage == 1:
            plane_arrived(s, near)
            plane_arrived(s, then)
        elif stage == 2:
            plane_arrived(s, across)
        else:
            for b in (1, 3, 5, 7):
                plane_arrived(s, flipped(r, b))
            return
        for hop in hops[stage]:
            plane_hop(s, hop).start()

    def ranks_hop(b):
        return remote(
            paux.at[r], paux.at[r], pas_sem.at[b], par_sem.at[r], at(0, b)
        )

    for k in range(1, planes):
        straight(*line_ranks, k).start()
    pltpu.make_async_copy(zbuf.at[0, z], zbuf.at[0, z], own_sem.at[0]).wait()
    for k in range(1, planes):
        first_straight(k).start()
    for b in range(1, PLANE):
        ranks_hop(b).start()
    plane_stage(0, 0)
    line_own(0, 1)
    for s in range(1, supers):
        plane_stage(s, 0)

    token = lax.broadcasted_iota(jnp.int32, (part, planes * tok), 1).astype(F32)
    token_z = jnp.floor((token + 0.5) * (1.0 / tok))
    _, slot_z, place = slot_numbers((part, planes * tok), 0, cap, planes)
    same_z = token_z == slot_z
    lane = lax.broadcasted_iota(jnp.int32, (part, LANES), 1)
    expert = slot_numbers((part, LANES), 0, cap, planes)[0].astype(jnp.int32)
    straight_arrived(*line_ranks)
    ranks = zrank[...].reshape(planes * tok, LANES)

    @pl.loop(0, PLANE)
    def _(p):
        first = (z * PLANE + p) * owned
        spread = jnp.where(lane == expert + first, 1.0, 0.0).astype(BF)
        rank_of = dot_t(spread, ranks)
        rows = pl.ds(pl.multiple_of(p * part, 16), part)
        choose_line[rows, :] = jnp.where(same_z & (rank_of == place), 1.0, 0.0).astype(BF)

    def choose_in_plane():
        for b in range(1, PLANE):
            other = flipped(r, b)
            remote(
                paux.at[other], paux.at[other], pas_sem.at[0], par_sem.at[other], at(0, 1)
            ).wait_recv()
        token = lax.broadcasted_iota(jnp.int32, (part_plane, PLANE * tok), 1).astype(F32)
        token_from = jnp.floor((token + 0.5) * (1.0 / tok))
        _, slot_from, place = slot_numbers((part_plane, PLANE * tok), 0, cap, PLANE)
        same = token_from == slot_from
        lane = lax.broadcasted_iota(jnp.int32, (part_plane, LANES), 1)
        expert = slot_numbers((part_plane, LANES), 0, cap, PLANE)[0].astype(jnp.int32)
        ranks = paux[...].reshape(PLANE * tok, LANES)

        @pl.loop(0, planes)
        def _(k):
            first = (k * PLANE + r) * owned
            spread = jnp.where(lane == expert + first, 1.0, 0.0).astype(BF)
            rank_of = dot_t(spread, ranks)
            rows = pl.ds(pl.multiple_of(k * part_plane, 16), part_plane)
            choose_plane[rows, :] = jnp.where(same & (rank_of == place), 1.0, 0.0).astype(BF)


    def line_give(a, b):
        other = flipped(r, b)
        slot = lax.rem(a, ring)
        return remote(
            packed_line.at[slot, other], xline.at[a, r], ls_sem.at[slot, other], lr_sem.at[a, r],
            at(0, b),
        )

    def line_keep(a):
        return pltpu.make_async_copy(
            packed_line.at[lax.rem(a, ring), r], xline.at[a, r], keep_sem.at[a]
        )

    def pack_line(a):
        line_rest(data, (a,))

        @pl.when(a == 0)
        def _():
            for k in forwarded:
                line_arrived(*data, (0,), k)

        @pl.when(a >= ring)
        def _():
            for b in range(1, PLANE):
                line_give(a - ring, b).wait_send()

        picked = dot(choose_line[...], zbuf[a].reshape(planes * tok, cw)).astype(BF)
        packed_line[lax.rem(a, ring)] = picked.reshape(PLANE, part, cw)
        for b in (2, 4, 6, 3, 5, 7, 1):
            line_give(a, b).start()
        line_keep(a).start()

    def plane_give(s, k):
        other = flipped(z, k)
        return remote(
            packed_plane.at[s, other], xplane.at[s, z], bs_sem.at[s, k], br_sem.at[s, z], at(k, 0)
        )

    def plane_keep(s):
        return pltpu.make_async_copy(packed_plane.at[s, z], xplane.at[s, z], bs_sem.at[s, 0])

    def pack_plane(s):
        picked = dot(choose_plane[...], pbuf[s].reshape(PLANE * tok, cw)).astype(BF)
        packed_plane[s] = picked.reshape(planes, part_plane, cw)
        for k in range(1, planes):
            plane_give(s, k).start()
        plane_keep(s).start()

    def rows_line(a):
        line_keep(a).wait()
        for b in range(1, PLANE):
            other = flipped(r, b)
            remote(
                xline.at[a, other], xline.at[a, other], ls_sem.at[0, 0], lr_sem.at[a, other],
                at(0, 1),
            ).wait_recv()
        return [
            xline[a, :, j * group:(j + 1) * group, :].reshape(PLANE * group, cw)
            for j in range(owned)
        ]

    def rows_plane(s):
        plane_keep(s).wait()
        for k in range(1, planes):
            other = flipped(z, k)
            remote(
                xplane.at[s, other], xplane.at[s, other], bs_sem.at[s, 0], br_sem.at[s, other],
                at(1, 0),
            ).wait_recv()
        return [
            dot(
                reorder[...],
                xplane[s, :, j * wide:(j + 1) * wide, :].reshape(PLANE * group, cw),
            ).astype(BF)
            for j in range(owned)
        ]

    def compute(s, i):
        n = 4 * s + i
        slot = i % 2
        rows = rows_plane(s) if i == 2 else rows_line(line_index(s, i))

        @pl.when(n + 1 < half)
        def _():
            for load in first_loads(n + 1, 1 - slot):
                load.start()

        @pl.when((n + 1 >= half) & (n + 1 < steps))
        def _():
            down_load(n + 1, 1 - slot).start()

        @pl.when(n + 1 == steps)
        def _():
            for load in first_loads(0, 1 - slot):
                load.start()

        if i == half % 4:
            @pl.when(n == half)
            def _():
                activate()

        @pl.when(n < half)
        def _():
            for load in first_loads(n, slot):
                load.wait()
            for j in range(owned):
                gate_acc[j] += dot(rows[j], gate_w[slot, j])
                up_acc[j] += dot(rows[j], up_w[slot, j])

        @pl.when(n >= half)
        def _():
            down_load(n, slot).wait()
            for j in range(owned):
                down_acc[j] += dot_t(rows[j], down_w[slot, j])

    def activate():
        @pl.loop(0, PLANE)
        def _(p):
            rows = pl.ds(pl.multiple_of(p * group, 16), group)
            for j in range(owned):
                gate_pre = gate_acc[j, rows, :]
                sigma = 1.0 / (1.0 + jnp.exp(-gate_pre))
                gate_acc[j, rows, :] = gate_pre * sigma
                slope[j, rows, :] = sigma * (1.0 + gate_pre * (1.0 - sigma))

    def mix(p):
        _, slot_z, place = slot_numbers((tok, part), 1, cap, planes)
        first = (z * PLANE + p) * owned
        spread = jnp.where(lane == expert + first, 1.0, 0.0).astype(BF)
        columns = slice(p * part, (p + 1) * part)
        for k in range(planes):
            rows = slice(k * tok, (k + 1) * tok)
            values = zamount[k]
            rank_of = dot_t(zrank[k], spread)
            hit = (rank_of == place) & (slot_z == float(k))
            marks[rows, columns] = jnp.where(hit, 1.0, 0.0).astype(BF)
            high = dot_t(values[:, :LANES], spread)
            low = dot_t(values[:, LANES:], spread)
            mix_high[rows, columns] = jnp.where(hit, high, 0.0).astype(BF)
            mix_low[rows, columns] = jnp.where(hit, low, 0.0).astype(BF)

    @pl.loop(0, supers + 2)
    def _(s):
        for i in range(4):
            @pl.when(s < supers)
            def _():
                if i == 2:
                    @pl.when(s == 0)
                    def _():
                        choose_in_plane()

                    plane_stage(s, 3)
                    pack_plane(s)
                else:
                    early = {0: ((0, 3), (1, 0)), 1: ((1, 1), (1, 3)), 3: ((2, 0), (2, 1))}[i]
                    later = {0: (s + 1, 3), 1: (s + 2, 0), 3: (s + 2, 1)}[i]
                    follow = {0: (s, 3), 1: (s + 1, 0), 3: (s + 1, 1)}[i]

                    @pl.when(s == 0)
                    def _():
                        for item in early:
                            if item[0] < supers:
                                line_own(*item)

                    @pl.when((s >= 1) & (later[0] < supers))
                    def _():
                        line_own(*later)

                    pack_line(line_index(s, i))

                    if i == 0:
                        @pl.when(s == 0)
                        def _():
                            for k in range(1, planes):
                                straight(*line_amounts, k).start()
                            line_forward(data, (1,))

                    @pl.when(follow[0] < supers)
                    def _():
                        line_forward(data, (line_index(*follow),))
                if i == 0:
                    @pl.when(s == 0)
                    def _():
                        for stage in (1, 2):
                            plane_stage(0, stage)
                if i == 2:
                    @pl.when(s == 0)
                    def _():
                        for stage in (1, 2):
                            for other in range(1, supers):
                                plane_stage(other, stage)

            for p in range(PLANE):
                if p % 4 == i:
                    @pl.when(s == 1 + p // 4)
                    def _():
                        if p == 0:
                            straight_arrived(*line_amounts)
                        mix(p)

            back, at_step = (i - lag) // 4, (i - lag) % 4

            @pl.when((s + back >= 0) & (s + back < supers))
            def _():
                compute(s + back, at_step)

    column = lax.broadcasted_iota(jnp.int32, (group, LANES), 1)

    @pl.loop(0, PLANE)
    def _(p):
        rows = pl.ds(pl.multiple_of(p * group, 16), group)
        for j in range(owned):
            mine = slice(j * group, (j + 1) * group)
            silu_val, up_pre, upward = gate_acc[j, rows, :], up_acc[j, rows, :], down_acc[j, rows, :]
            up_delta = upward * silu_val
            pick_gate = jnp.sum(up_delta * up_pre, axis=1, keepdims=True)
            gate_delta = upward * up_pre * slope[j, rows, :]
            for d in range(deltas):
                columns = slice(d * cw, (d + 1) * cw)
                xline[d, p, mine, :] = gate_delta[:, columns].astype(BF)
                xline[deltas + d, p, mine, :] = up_delta[:, columns].astype(BF)
            high = pick_gate.astype(BF).astype(F32)
            low = pick_gate - high
            both = jnp.where(column == 0, high, jnp.where(column == 1, low, 0.0))
            gsend[p, mine, :] = both.astype(BF)

    @pl.loop(supers * 3 - ring, supers * 3)
    def _(a):
        for b in range(1, PLANE):
            line_give(a, b).wait_send()

    for k in range(1, planes):
        first_straight(k).wait_send()

    @pl.loop(1, 3 * supers)
    def _(a):
        for e in range(len(edges)):
            line_hop(*data, (a,), e).wait_send()

    returns = half

    def give(c, b):
        return remote(
            packed_line.at[c, flipped(r, b)], rrecv.at[c, r], rs_sem.at[c, b], rr_sem.at[c, r],
            at(0, b),
        )

    def keep(c):
        return pltpu.make_async_copy(packed_line.at[c, r], rrecv.at[c, r], rs_sem.at[c, 0])

    def give_gate(b):
        return remote(
            gsend.at[flipped(r, b)], grecv.at[r], gs_sem.at[b], gr_sem.at[r], at(0, b)
        )

    keep_gate = pltpu.make_async_copy(gsend.at[r], grecv.at[r], gs_sem.at[0])

    def home(c, k):
        slot = flipped(z, k)
        return remote(
            zbuf.at[c, slot], zrecv.at[c, z], hs_sem.at[c, k], hr_sem.at[c, z], at(k, 0)
        )

    def home_gate(k):
        slot = flipped(z, k)
        return remote(
            zgsend.at[slot], zgrecv.at[z], hgs_sem.at[k], hgr_sem.at[z], at(k, 0)
        )

    for b in range(1, PLANE):
        give_gate(b).start()
    keep_gate.start()

    def produce(c):
        slot = lax.rem(c, 2)

        @pl.when(c + 1 < returns)
        def _():
            for load in first_loads(c + 1, 1 - slot):
                load.start()

        for load in first_loads(c, slot):
            load.wait()
        for j in range(owned):
            mine = slice(j * group, (j + 1) * group)
            total = None
            for d in range(2 * deltas):
                weight = gate_w if d < deltas else up_w
                columns = slice((d % deltas) * cw, (d % deltas + 1) * cw)
                rows = xline[d, :, mine, :].reshape(PLANE * group, cw)
                term = dot_t(rows, weight[slot, j, :, columns])
                total = term if total is None else total + term
            packed_line[c, :, mine, :] = total.astype(BF).reshape(PLANE, group, cw)
        for b in (2, 4, 6, 3, 5, 7, 1):
            give(c, b).start()
        keep(c).start()

    own = pl.ds(pl.multiple_of(z * tok, tok), tok)

    def merge(c):
        keep(c).wait()
        for b in range(1, PLANE):
            other = flipped(r, b)
            remote(
                rrecv.at[c, other], rrecv.at[c, other], rs_sem.at[c, 0], rr_sem.at[c, other],
                at(0, 1),
            ).wait_recv()
        rows = rrecv[c].reshape(slots, cw)
        total = dot(mix_high[...], rows) + dot(mix_low[...], rows)
        zbuf[c] = total.astype(BF).reshape(planes, tok, cw)
        for k in range(1, planes):
            home(c, k).start()
        columns = pl.ds(pl.multiple_of(c * cw, cw), cw)
        out_ref[:, columns] = dot(mix_high[own, :], rows) + dot(mix_low[own, :], rows)

        @pl.when(c == 1)
        def _():
            keep_gate.wait()
            for b in range(1, PLANE):
                other = flipped(r, b)
                remote(
                    grecv.at[other], grecv.at[other], gs_sem.at[0], gr_sem.at[other], at(0, 1)
                ).wait_recv()
            picked = grecv[...].reshape(slots, LANES).astype(F32)
            lane_of = lax.broadcasted_iota(jnp.int32, (slots, LANES), 1)
            number = slot_numbers((slots, LANES), 0, cap, planes)[0].astype(jnp.int32)
            here = lane_of == number + z * PLANE * owned
            high = jnp.sum(jnp.where(lane_of == 0, picked, 0.0), axis=1, keepdims=True)
            low = jnp.sum(jnp.where(lane_of == 1, picked, 0.0), axis=1, keepdims=True)
            high = jnp.where(here, high, 0.0).astype(BF)
            low = jnp.where(here, low, 0.0).astype(BF)
            gates = dot(marks[...], high) + dot(marks[...], low)
            zgsend[...] = gates.reshape(planes, tok, LANES)
            for k in range(1, planes):
                home_gate(k).start()

    def finish(c):
        columns = pl.ds(pl.multiple_of(c * cw, cw), cw)
        total = out_ref[:, columns]
        for k in range(1, planes):
            slot = flipped(z, k)
            remote(
                zrecv.at[c, slot], zrecv.at[c, slot], hs_sem.at[c, 0], hr_sem.at[c, slot],
                at(1, 0),
            ).wait_recv()
            total = total + zrecv[c, slot].astype(F32)
        out_ref[:, columns] = total

    @pl.loop(0, returns + BEHIND + LAST)
    def _(t):
        @pl.when(t < returns)
        def _():
            produce(t)

        @pl.when((t >= BEHIND) & (t < returns + BEHIND))
        def _():
            merge(t - BEHIND)

        @pl.when(t >= BEHIND + LAST)
        def _():
            finish(t - BEHIND - LAST)

    total = zgsend[z]
    for k in range(1, planes):
        slot = flipped(z, k)
        remote(
            zgrecv.at[slot], zgrecv.at[slot], hgs_sem.at[0], hgr_sem.at[slot], at(1, 0)
        ).wait_recv()
        total = total + zgrecv[slot]
    total = total.T
    for k in range(top):
        hit = expert_row == ids_ref[k:k + 1, :]
        gate_out[k:k + 1, :] = jnp.sum(jnp.where(hit, total, 0.0), axis=0, keepdims=True)

    for k in range(1, planes):
        straight(*line_ranks, k).wait_send()
        straight(*line_amounts, k).wait_send()
    for b in range(1, PLANE):
        ranks_hop(b).wait_send()
        give_gate(b).wait_send()
    for k in range(1, planes):
        home_gate(k).wait_send()

    @pl.loop(0, supers)
    def _(s):
        for stage in hops:
            for hop in stage:
                plane_hop(s, hop).wait_send()
        for k in range(1, planes):
            plane_give(s, k).wait_send()

    @pl.loop(0, returns)
    def _(c):
        for b in range(1, PLANE):
            give(c, b).wait_send()
        for k in range(1, planes):
            home(c, k).wait_send()


def fused(planes, cap, tokens, cotangent, weights, ids, gate_weight, up_weight, down_weight):
    tok, width = tokens.shape
    owned, _, ff = gate_weight.shape
    cw = COLUMNS
    half = width // cw
    supers = 2 * half // 4
    line = 3 * supers
    ring = half
    group = planes * cap
    part, rows = owned * group, PLANE * group
    part_plane = owned * PLANE * cap
    slots = PLANE * part
    edges = len(line_edges(planes))
    vmem = pl.BlockSpec(memory_space=pltpu.VMEM)
    hbm = pl.BlockSpec(memory_space=pl.ANY)
    dma = pltpu.SemaphoreType.DMA
    return pl.pallas_call(
        functools.partial(fused_kernel, planes, cap, ring, 5),
        out_shape=(
            jax.ShapeDtypeStruct((tok, width), F32),
            jax.ShapeDtypeStruct(ids.shape, F32),
        ),
        in_specs=[hbm, hbm, vmem, vmem, hbm, hbm, hbm],
        out_specs=(vmem, vmem),
        scratch_shapes=[
            pltpu.VMEM((line, planes, tok, cw), BF),
            pltpu.VMEM((supers, PLANE, tok, cw), BF),
            pltpu.VMEM((planes, tok, LANES), BF),
            pltpu.VMEM((planes, tok, 2 * LANES), BF),
            pltpu.VMEM((PLANE, tok, LANES), BF),
            pltpu.VMEM((PLANE * part, planes * tok), BF),
            pltpu.VMEM((planes * part_plane, PLANE * tok), BF),
            pltpu.VMEM((rows, rows), BF),
            pltpu.VMEM((ring, PLANE, part, cw), BF),
            pltpu.VMEM((supers, planes, part_plane, cw), BF),
            pltpu.VMEM((line, PLANE, part, cw), BF),
            pltpu.VMEM((supers, planes, part_plane, cw), BF),
            pltpu.VMEM((owned, rows, ff), F32),
            pltpu.VMEM((owned, rows, ff), F32),
            pltpu.VMEM((owned, rows, ff), F32),
            pltpu.VMEM((owned, rows, ff), F32),
            pltpu.VMEM((2, owned, cw, ff), BF),
            pltpu.VMEM((2, owned, cw, ff), BF),
            pltpu.VMEM((2, owned, ff, cw), BF),
            pltpu.VMEM((half, PLANE, part, cw), BF),
            pltpu.VMEM((PLANE, part, LANES), BF),
            pltpu.VMEM((PLANE, part, LANES), BF),
            pltpu.VMEM((planes * tok, slots), BF),
            pltpu.VMEM((planes * tok, slots), BF),
            pltpu.VMEM((planes * tok, slots), BF),
            pltpu.VMEM((half, planes, tok, cw), BF),
            pltpu.VMEM((planes, tok, LANES), F32),
            pltpu.VMEM((planes, tok, LANES), F32),
            dma((3, 2)),
            dma((4 * supers,)),
            dma((planes,)),
            dma((planes,)),
            dma((planes,)),
            dma((planes,)),
            dma((PLANE,)),
            dma((PLANE,)),
            dma((line, edges)),
            dma((line, planes)),
            dma((supers, 7)),
            dma((supers, PLANE)),
            dma((ring, PLANE)),
            dma((line, PLANE)),
            dma((supers, planes)),
            dma((supers, planes)),
            dma((line,)),
            dma((half, PLANE)),
            dma((half, PLANE)),
            dma((PLANE,)),
            dma((PLANE,)),
            dma((half, planes)),
            dma((half, planes)),
            dma((planes,)),
            dma((planes,)),
        ],
        compiler_params=pltpu.CompilerParams(
            collective_id=0, has_side_effects=True, vmem_limit_bytes=62 * 2**20
        ),
    )(tokens, cotangent, weights, ids, gate_weight, up_weight, down_weight)


def by_planes(planes, tokens, cotangent, routing, expert_ids, gate_weight, up_weight, down_weight):
    owned = gate_weight.shape[0]
    experts = owned * planes * PLANE
    tok, top = expert_ids.shape
    cap = 5 * tok * top // (4 * experts)
    input_grad, gate_grad = fused(
        planes, cap, tokens, cotangent, routing.T, expert_ids.T, gate_weight, up_weight,
        down_weight,
    )
    return input_grad, gate_grad.T


def local(tokens, cotangent, routing, expert_ids, gate_weight, up_weight, down_weight):
    count = lax.axis_size("ep")
    owned = gate_weight.shape[0]
    experts = owned * count
    tok_rows, top = expert_ids.shape
    width = tokens.shape[1]
    cap = 5 * tok_rows * top // (4 * experts)
    slots = experts * cap

    onehot = expert_ids[:, :, None] == jnp.arange(experts, dtype=jnp.int32)[None, None, :]
    picked = jnp.any(onehot, axis=1)
    row = jnp.arange(tok_rows, dtype=jnp.int32)
    lower = (row[:, None] > row[None, :]).astype(BF)
    before = dot(lower, picked.astype(BF))
    rank = jnp.where(picked, before, -1.0).astype(BF)
    slot = jnp.arange(slots, dtype=jnp.int32)
    spread = (slot[:, None] // cap == jnp.arange(experts, dtype=jnp.int32)[None, :]).astype(BF)
    place = (slot % cap).astype(F32)
    rank_of = lax.dot_general(spread, rank, (((1,), (1,)), ((), ())), preferred_element_type=F32)
    choose = (rank_of == place[:, None]).astype(BF)
    rank_back = lax.dot_general(rank, spread, (((1,), (1,)), ((), ())), preferred_element_type=F32)
    choose_back = rank_back == place[None, :]

    def exchange(value):
        return lax.all_to_all(value, "ep", split_axis=0, concat_axis=0, tiled=True)

    def by_expert(value):
        value = value.reshape(count, owned, cap, value.shape[1])
        return value.transpose(1, 0, 2, 3).reshape(owned, count * cap, value.shape[3])

    def by_source(value):
        value = value.reshape(owned, count, cap, value.shape[2])
        return value.transpose(1, 0, 2, 3).reshape(slots, value.shape[3])

    inputs = by_expert(exchange(dot(choose, tokens).astype(BF)))
    grads_in = by_expert(exchange(dot(choose, cotangent).astype(BF)))
    gate_pre = jnp.einsum("erd,edf->erf", inputs, gate_weight, preferred_element_type=F32)
    up_pre = jnp.einsum("erd,edf->erf", inputs, up_weight, preferred_element_type=F32)
    upward = jnp.einsum("erd,efd->erf", grads_in, down_weight, preferred_element_type=F32)
    sigma = jax.nn.sigmoid(gate_pre)
    silu_val = gate_pre * sigma
    pick_gate = jnp.sum(silu_val * up_pre * upward, axis=2, keepdims=True)
    gate_delta = (upward * up_pre * sigma * (1.0 + gate_pre * (1.0 - sigma))).astype(BF)
    up_delta = (upward * silu_val).astype(BF)
    deltas = jnp.concatenate([gate_delta, up_delta], axis=2)
    joined = jnp.concatenate([gate_weight, up_weight], axis=2)

    half = width // 2
    gate_high, gate_low = split_two(pick_gate)
    lane = jnp.arange(128, dtype=jnp.int32)[None, None, :]
    gate_cols = jnp.where(lane == 0, gate_high, jnp.where(lane == 1, gate_low, jnp.zeros((), BF)))
    first = jnp.einsum("erf,edf->erd", deltas, joined[:, :half], preferred_element_type=F32).astype(BF)
    second = jnp.einsum("erf,edf->erd", deltas, joined[:, half:], preferred_element_type=F32).astype(BF)
    back_a = exchange(by_source(jnp.concatenate([first, gate_cols], axis=2)))
    back_b = exchange(by_source(second))

    amount = jnp.sum(jnp.where(onehot, routing[:, :, None], 0.0), axis=1)
    amount_high, amount_low = split_two(amount)
    zero = jnp.zeros((), BF)

    def mix(part):
        wide = lax.dot_general(part, spread, (((1,), (1,)), ((), ())), preferred_element_type=F32)
        return jnp.where(choose_back, wide.astype(BF), zero)

    mixing = jnp.concatenate([mix(amount_high), mix(amount_low)], axis=0)

    def combine(value):
        both = dot(mixing, value)
        return both[:tok_rows] + both[tok_rows:]

    weighted = jnp.concatenate([combine(back_a[:, :half]), combine(back_b)], axis=1)
    gates = back_a[:, half:half + 2].T

    def gate_part(i):
        return dot(jnp.where(choose_back, gates[i][None, :], zero), spread)

    gate_sum = gate_part(0) + gate_part(1)
    gate_grad = jnp.sum(jnp.where(onehot, gate_sum[:, None, :], 0.0), axis=2)
    input_grad = lax.psum_scatter(weighted, "hid", scatter_dimension=1, tiled=True)
    return (input_grad, lax.psum(gate_grad, "hid"))


def solution(mesh):
    placed = (
        P(("rep", "ep"), None),
        P(("rep", "ep"), None),
        P(("rep", "ep"), None),
        P(("rep", "ep"), None),
        P("ep", None, "hid"),
        P("ep", None, "hid"),
        P("ep", "hid", None),
    )
    count = mesh.shape["ep"]
    planes = count // PLANE
    direct = (
        mesh.shape["rep"] * mesh.shape["hid"] == 1
        and count % PLANE == 0
        and planes > 1
        and planes & (planes - 1) == 0
    )

    def run(tokens, cotangent, routing, expert_ids, gate_weight, *rest):
        tok, top = expert_ids.shape
        owned, width, ff = gate_weight.shape
        cap = 5 * tok * top // (4 * owned * count)
        fits = (
            direct
            and owned * count <= LANES
            and planes * cap % 16 == 0
            and tok % LANES == 0
            and width % (4 * COLUMNS) == 0
            and ff % COLUMNS == 0
            and 2 * ff // COLUMNS <= 6 * width // (4 * COLUMNS)
        )
        body = functools.partial(by_planes, planes) if fits else local
        return body(tokens, cotangent, routing, expert_ids, gate_weight, *rest)

    return jax.shard_map(
        run,
        mesh=mesh,
        in_specs=placed,
        out_specs=(P(("rep", "ep"), "hid"), P(("rep", "ep"), None)),
        check_vma=False,
    )
```
